32 devices in a mesh: section: 2 (over x), expert: 4 (over z), replica: 4 (over y, core).
Axes of the slice: x: 2, y: 2, z: 4, core: 2. Of those that a mesh axis runs over, the one named last changes fastest.
Arguments:
- inputs: bfloat16 [2, 4, 1024, 1024], P(None, 'expert', 'replica'), may hold values from -8 to 8
- cotangent: bfloat16 [2, 4, 1024, 1024], P(None, 'expert', 'replica'), may hold values from -6 to 6
- routes: int32 [2, 2, 4, 1024, 2], P('section', None, 'expert', 'replica'), may hold values from 0 to 3, all different within a row; in each aligned block of 256 rows (0 to 255, 256 to 511, ..., all dimensions but the last counted through in order) at most 144 rows name the same one
- bucket_table: int32 [2047], replicated, may hold values from 0 to 31
- query_weight: bfloat16 [2, 1024, 1024], P('section', 'expert'), may hold values from -0.1875 to 0.1875
- key_weight: bfloat16 [2, 1024, 1024], P('section', 'expert'), may hold values from -0.1875 to 0.1875
- value_weight: bfloat16 [2, 1024, 1024], P('section', 'expert'), may hold values from -0.1875 to 0.1875
- output_weight: bfloat16 [2, 1024, 1024], P('section', 'expert'), may hold values from -2 to 2
- router_weight: bfloat16 [2, 1024, 4], P('section', 'expert'), may hold values from -0.1875 to 0.1875
- attention_gain: bfloat16 [2, 1024], P('section', 'expert'), may hold values from 0.25 to 1.75
- mixture_gain: bfloat16 [2, 1024], P('section', 'expert'), may hold values from 0.25 to 1.75
- position_bias: bfloat16 [2, 16, 32], P('section', 'expert'), may hold values from -4 to 4
- expert_gate: bfloat16 [2, 4, 1024, 2816], P('section', 'expert', 'replica'), may hold values from -0.1875 to 0.1875
- expert_up: bfloat16 [2, 4, 1024, 2816], P('section', 'expert', 'replica'), may hold values from -0.1875 to 0.1875
- expert_down: bfloat16 [2, 4, 2816, 1024], P('section', 'expert', None, 'replica'), may hold values from -0.4375 to 0.4375
Outputs:
- section_output: bfloat16 [2, 2, 4, 1024, 1024], P('section', None, 'expert', 'replica')
- input_gradient: float32 [2, 2, 4, 1024, 1024], P('section', None, 'expert', 'replica')
- gradient_query: float32 [2, 1024, 1024], P('section', 'expert')
- gradient_key: float32 [2, 1024, 1024], P('section', 'expert')
- gradient_value: float32 [2, 1024, 1024], P('section', 'expert')
- gradient_output: float32 [2, 1024, 1024], P('section', 'expert')
- gradient_router: float32 [2, 1024, 4], P('section', 'expert')
- gradient_attention_gain: float32 [2, 1024], P('section', 'expert')
- gradient_mixture_gain: float32 [2, 1024], P('section', 'expert')
- gradient_position: float32 [2, 16, 32], P('section', 'expert')
- gradient_expert_gate: float32 [2, 4, 1024, 2816], P('section', 'expert', 'replica')
- gradient_expert_up: float32 [2, 4, 1024, 2816], P('section', 'expert', 'replica')
- gradient_expert_down: float32 [2, 4, 2816, 1024], P('section', 'expert', None, 'replica')
The draws below stay inside these ranges and needn't reach their ends.
Inputs may be any that keep to these rules, and one draw needn't show every extreme that they name: `routes`: each token names two different experts. Among the 256 tokens of one block (one device's rows of one micro-batch) no expert is named more than 144 times, a bound that some block reaches.
All inputs are finite; a program needn't handle non-finite values.
Results may differ from the reference program's by a relative error of at most 0.023.
Values may be sent and summed in bfloat16 or wider, within the bound.
No kernel may reach another device: no remote copies, remote signals or barrier semaphores. Data moves between devices by JAX's collectives and lax.ppermute only.
A program may use at most 512 MiB of HBM per device.

```python
import math
import jax
import jax.numpy as jnp
import numpy as np
from jax import lax

D = 1024
HEADS = 16
HEAD_DIM = 64
FF = 2816
BUCKETS = 32
TOK_MB = 256
MICRO = 2
EXPERTS = 4
SEQS = 4
LENGTH = 1024
CAP = 144
N_REPLICA = 4


def draw_inputs(key, part):
    noise_key = jax.random.fold_in(key, 11)
    common_key = jax.random.fold_in(key, 23)
    noise = jax.random.normal(noise_key, (MICRO, SEQS, LENGTH, D), jnp.float32)
    common = jax.random.normal(common_key, (MICRO, SEQS, 1, D), jnp.float32)
    return jnp.clip(noise + common, -8.0, 8.0).astype(jnp.bfloat16)


def touch_ends(drawn, rng, smallest, high):
    spot = [jax.random.randint(jax.random.fold_in(rng, axis), (), 0, length) for axis, length in enumerate(drawn.shape)]
    widest = drawn.shape.index(max(drawn.shape))
    neighbour = spot[:widest] + [(spot[widest] + 1) % drawn.shape[widest]] + spot[widest + 1:]
    return drawn.at[tuple(spot)].set(smallest).at[tuple(neighbour)].set(high)


def steps_of(own_key, extent, cuts, low, top_value):
    level = 1.0
    for dim, parts in cuts:
        steps = jax.random.uniform(jax.random.fold_in(jax.random.fold_in(own_key, 6), dim), (parts,), jnp.float32, low / len(cuts), top_value / len(cuts))
        level = level * jnp.repeat(jnp.exp(steps), extent[dim] // parts).reshape((-1,) + (1,) * (len(extent) - 1 - dim))
    return level


def shared_out(stream_key, own, number, rows, amount, top, limit, skew):
    ranking = jax.random.permutation(stream_key, amount)
    crowded, usual = load_shares(amount, rows * top, limit, skew, True), load_shares(amount, rows * top, limit, skew, False)
    places = jnp.arange(amount)

    def named(tallies, rotation):
        used = int((tallies > 0).sum())
        fixed = max(1, used // 4)
        moved = fixed + (places - fixed + rotation * (used - fixed)) % max(1, amount - fixed)
        return jnp.zeros((amount,), jnp.int32).at[ranking[jnp.where(places < fixed, places, moved)]].set(jnp.asarray(tallies, jnp.int32))

    tallies = jnp.where(number % 4 == 0, named(crowded, number // 4), named(usual, number - number // 4 - 1))
    mixed = jax.random.permutation(jax.random.fold_in(own, 3), amount)
    donor, receiver = mixed[0:amount // 2 * 2:2], mixed[1:amount // 2 * 2:2]
    slack = jnp.minimum(tallies[donor] - 1, limit - tallies[receiver]) // 2
    slack = jnp.where((donor == ranking[0]) | (receiver == ranking[0]) | (tallies[receiver] == 0), 0, jnp.maximum(slack, 0))
    moved = jax.random.randint(jax.random.fold_in(own, 4), (amount // 2,), 0, 1 << 20) % (slack + 1)
    tallies = tallies.at[donor].add(-moved).at[receiver].add(moved)
    items = jnp.searchsorted(jnp.cumsum(tallies), jnp.arange(rows * top), side="right").astype(jnp.int32)
    listing = items.reshape(top, rows).T
    listing = listing[jax.random.permutation(jax.random.fold_in(own, 1), rows)]
    rotation = jax.random.randint(jax.random.fold_in(own, 2), (rows, 1), 0, top)
    return jnp.take_along_axis(listing, (jnp.arange(top)[None, :] + rotation) % top, axis=1)


def load_shares(amount, total, most, slope, full):
    loads = [(1 << 20) // math.isqrt(standing ** slope) + 1 for standing in range(1, amount + 1)]
    largest = most if full else min(most, max(-(-total // amount), total * loads[0] // sum(loads)))
    least = 1 if total - largest >= amount - 1 else 0
    counts, spare = [largest] + [least] * (amount - 1), total - largest - least * (amount - 1)
    while spare > 0:
        candidates = [i for i in range(1, amount) if counts[i] < largest] or [i for i in range(1, amount) if counts[i] < most]
        whole, left = sum([loads[i] for i in candidates]), spare
        for i in candidates:
            addition = min(most - counts[i], max(1, left * loads[i] // whole), spare)
            counts[i] = counts[i] + addition
            spare = spare - addition
    return np.array(counts)


def scatter_about(own_key, extent, width, bound, pieces=(), kind=jnp.bfloat16):
    loudness = steps_of(own_key, extent, pieces, -0.22, 0.18) if pieces else 1.0
    drawn = jax.random.normal(own_key, extent, jnp.float32) * width * loudness
    return jnp.minimum(jnp.maximum(drawn, -bound), bound).astype(kind)


def setup_inputs(seed: int = 0) -> dict:
    keys = jax.random.split(jax.random.key(seed), 16)
    inputs = draw_inputs(jax.random.fold_in(keys[15], 71), 0)
    cotangent = scatter_about(keys[1], (MICRO, SEQS, LENGTH, D), 1.0, 6.0, ((1, 4), (2, 4)))
    routes_keys = jax.random.split(jax.random.fold_in(keys[2], 1), 2 * MICRO * SEQS * LENGTH // TOK_MB)
    routes_turns = jax.random.permutation(jax.random.fold_in(keys[2], 3), 2 * MICRO * SEQS * LENGTH // TOK_MB)
    routes = jax.vmap(lambda own, number: shared_out(jax.random.fold_in(keys[2], 2), own, number, TOK_MB, EXPERTS, 2, CAP, 2))(routes_keys, routes_turns).reshape((2, MICRO, SEQS, LENGTH, 2))
    bucket_table = touch_ends(jax.random.randint(keys[3], (2 * LENGTH - 1,), 0, BUCKETS), jax.random.fold_in(keys[3], 1), 0, BUCKETS - 1).astype(jnp.int32)
    query_weight = scatter_about(keys[4], (2, D, D), D ** -0.5, 0.1875, ((0, 2), (1, 4)))
    key_weight = scatter_about(keys[5], (2, D, D), D ** -0.5, 0.1875, ((0, 2), (1, 4)))
    value_weight = scatter_about(keys[6], (2, D, D), D ** -0.5, 0.1875, ((0, 2), (1, 4)))
    output_weight = scatter_about(keys[7], (2, D, D), (max(1, (8 * D) // LENGTH)) ** -0.5, 2.0, ((0, 2), (1, 4)))
    router_weight = scatter_about(keys[8], (2, D, EXPERTS), D ** -0.5, 0.1875, ((0, 2), (1, 4)))
    attention_gain = jnp.clip(1.0 + 0.15 * jax.random.normal(keys[9], (2, D), jnp.float32), 0.25, 1.75).astype(jnp.bfloat16)
    mixture_gain = jnp.clip(1.0 + 0.15 * jax.random.normal(keys[10], (2, D), jnp.float32), 0.25, 1.75).astype(jnp.bfloat16)
    position_bias = scatter_about(keys[11], (2, HEADS, BUCKETS), 1.0, 4.0, ((0, 2), (1, 4)))
    expert_gate = scatter_about(keys[12], (2, EXPERTS, D, FF), D ** -0.5, 0.1875, ((0, 2), (1, 4), (2, 4)))
    expert_up = scatter_about(keys[13], (2, EXPERTS, D, FF), D ** -0.5, 0.1875, ((0, 2), (1, 4), (2, 4)))
    expert_down = scatter_about(keys[14], (2, EXPERTS, FF, D), (max(1, FF // (EXPERTS * EXPERTS))) ** -0.5, 0.4375, ((0, 2), (1, 4), (3, 4)))
    return dict(inputs=inputs, cotangent=cotangent, routes=routes, bucket_table=bucket_table, query_weight=query_weight, key_weight=key_weight, value_weight=value_weight, output_weight=output_weight, router_weight=router_weight, attention_gain=attention_gain, mixture_gain=mixture_gain, position_bias=position_bias, expert_gate=expert_gate, expert_up=expert_up, expert_down=expert_down)


EPSILON = 1e-06
HIGHEST = lax.Precision.HIGHEST

@jax.custom_vjp
def low(v):
    return lax.optimization_barrier(v.astype(jnp.bfloat16)).astype(jnp.float32)

@jax.custom_vjp
def low_back(v):
    return v

def low_keep(v):
    return (low(v), None)

def low_pass(kept, grad):
    return (grad,)

def back_keep(v):
    return (v, None)

def back_low(kept, grad):
    return (low(grad),)
low.defvjp(low_keep, low_pass)
low_back.defvjp(back_keep, back_low)

def matmul(left, right):
    return jnp.dot(left, right, precision=HIGHEST, preferred_element_type=jnp.float32)

def rms_scale(values, gain):
    return values * lax.rsqrt(lax.optimization_barrier(jnp.mean(values * values, axis=-1, keepdims=True)) + EPSILON) * gain

def softmax_rows(scores):
    row_top = lax.optimization_barrier(jnp.max(scores, axis=-1, keepdims=True))
    expos = jnp.exp(scores - row_top)
    return expos / lax.optimization_barrier(jnp.sum(expos, axis=-1, keepdims=True))

def attend_one(normed, weight_query, weight_key, weight_value, bias):
    length = normed.shape[0]
    queries = low_back(low(matmul(normed, weight_query))).reshape(length, HEADS, HEAD_DIM)
    keys_all = low_back(low(matmul(normed, weight_key))).reshape(length, HEADS, HEAD_DIM)
    values_all = low_back(low(matmul(normed, weight_value))).reshape(length, HEADS, HEAD_DIM)
    scores = jnp.einsum('qhd,khd->hqk', queries, keys_all, precision=HIGHEST) / math.sqrt(HEAD_DIM) + bias
    attention = softmax_rows(low_back(scores))
    mixed = jnp.einsum('hqk,khd->qhd', low(attention), values_all, precision=HIGHEST)
    return low_back(low(mixed.reshape(length, HEADS * HEAD_DIM)))

def expert_one(member):
    rows, weight_gate, weight_up, weight_down = member
    gate_part = low_back(matmul(rows, weight_gate))
    up_part = low_back(matmul(rows, weight_up))
    hidden = low(jax.nn.gelu(gate_part, approximate=True) * up_part)
    return low_back(low(matmul(hidden, weight_down)))

def section_layer(section_in, route, bucket_table, weight_query, weight_key, weight_value, weight_output, weight_router, gain_first, gain_second, position, weight_gate, weight_up, weight_down):
    micro, seqs, length, model_width = section_in.shape
    places = jnp.arange(length, dtype=jnp.int32)
    offsets = places[None, :] - places[:, None] + length - 1
    bias = jnp.take(jnp.take(position, bucket_table, axis=1), offsets, axis=1)
    normed = low(rms_scale(section_in, gain_first)).reshape(micro * seqs, length, model_width)
    attend = jax.checkpoint(lambda sequence: attend_one(sequence, weight_query, weight_key, weight_value, bias))
    attended = lax.map(attend, normed)
    branch = low_back(matmul(attended.reshape(-1, model_width), weight_output))
    middle = section_in + branch.reshape(section_in.shape)
    mixed_in = low(rms_scale(middle, gain_second))
    gates_all = softmax_rows(low_back(matmul(mixed_in.reshape(-1, model_width), weight_router)))
    blocks = (micro, seqs, N_REPLICA, TOK_MB)
    route_blocks = route.reshape(blocks + (2,))
    onehot = (route_blocks[..., None] == jnp.arange(EXPERTS, dtype=jnp.int32)).astype(jnp.int32)
    per_row = lax.optimization_barrier(jnp.sum(onehot, axis=-2))
    before = jnp.cumsum(per_row, axis=-2) - per_row
    slot_place = lax.optimization_barrier(jnp.sum(before[..., None, :] * onehot, axis=-1))
    target = route_blocks * CAP + slot_place
    spots = (target[..., None] == jnp.arange(EXPERTS * CAP, dtype=jnp.int32)).astype(jnp.float32)
    slot_table = lax.optimization_barrier(jnp.sum(spots, axis=-2))
    packed = jnp.einsum('mnrts,mnrtd->mnrsd', slot_table, mixed_in.reshape(blocks + (model_width,)), precision=HIGHEST)
    packed = packed.reshape(micro, seqs, N_REPLICA, EXPERTS, CAP, model_width)
    packed = low_back(packed.transpose(3, 0, 1, 2, 4, 5).reshape(EXPERTS, -1, model_width))
    produced = lax.map(jax.checkpoint(expert_one), (packed, weight_gate, weight_up, weight_down))
    produced = produced.reshape(EXPERTS, micro, seqs, N_REPLICA, CAP, model_width)
    produced = produced.transpose(1, 2, 3, 0, 4, 5).reshape(micro, seqs, N_REPLICA, EXPERTS * CAP, model_width)
    picked = jnp.take_along_axis(gates_all.reshape(blocks + (EXPERTS,)), route_blocks, axis=-1)
    combine = lax.optimization_barrier(jnp.sum(spots * picked[..., None], axis=-2))
    mixed_out = jnp.einsum('mnrts,mnrsd->mnrtd', combine, produced, precision=HIGHEST)
    result = middle + mixed_out.reshape(section_in.shape)
    return low(result)

def reference(inputs, cotangent, routes, bucket_table, query_weight, key_weight, value_weight, output_weight, router_weight, attention_gain, mixture_gain, position_bias, expert_gate, expert_up, expert_down):
    params = tuple((member.astype(jnp.float32) for member in (query_weight, key_weight, value_weight, output_weight, router_weight, attention_gain, mixture_gain, position_bias, expert_gate, expert_up, expert_down)))
    start = inputs.astype(jnp.float32)

    def forward(first, offset_in, weights):
        out_first = section_layer(first, routes[0], bucket_table, *[member[0] for member in weights])
        second = low_back(out_first) + offset_in
        out_second = section_layer(second, routes[1], bucket_table, *[member[1] for member in weights])
        return (out_first, out_second)
    primal, pull = jax.vjp(forward, start, jnp.zeros_like(start), params)
    out_first, out_second = primal
    grad_first, grad_second, grads = pull((jnp.zeros_like(out_first), cotangent.astype(out_second.dtype)))
    section_output = jnp.stack([out_first, out_second]).astype(jnp.bfloat16)
    input_gradient = jnp.stack([grad_first, grad_second])
    return (section_output, input_gradient, grads[0], grads[1], grads[2], grads[3], grads[4], grads[5], grads[6], grads[7], grads[8], grads[9], grads[10])
```

```python
import functools
import math

import jax
import jax.numpy as jnp
from jax import lax
from jax.experimental import pallas as pl
from jax.experimental.pallas import tpu as pltpu
from jax.sharding import Mesh
from jax.sharding import PartitionSpec as P

HEADS = 16
HEAD_DIM = 64
EPSILON = 1e-06
ROOT_SIZE = math.sqrt(HEAD_DIM)

SECTION = "section"
EXPERT = "expert"
OUTER = "outer"
INNER = "inner"
REPLICA = (OUTER, INNER)

BF16 = jnp.bfloat16
F32 = jnp.float32
ROWS = 128


def matmul(left, right):
    return jnp.dot(left, right, preferred_element_type=F32)


def dot_nt(left, right):
    return lax.dot_general(left, right, (((1,), (1,)), ((), ())), preferred_element_type=F32)


def dot_tn(left, right):
    return lax.dot_general(left, right, (((0,), (0,)), ((), ())), preferred_element_type=F32)


def rms_scale(values, gain):
    return values * lax.rsqrt(jnp.mean(values * values, axis=-1, keepdims=True) + EPSILON) * gain


def softmax_rows(scores):
    row_top = jnp.max(scores, axis=-1, keepdims=True)
    expos = jnp.exp(scores - row_top)
    return expos / jnp.sum(expos, axis=-1, keepdims=True)


def gated_gelu(gate_part, up_part):
    return jax.nn.gelu(gate_part, approximate=True) * up_part


def shift_to(value, axis, steps):
    count = lax.axis_size(axis)
    return lax.ppermute(value, axis, [(source, (source + steps) % count) for source in range(count)])


def bias_rows(window, half, queries):
    width = queries + ROWS
    start = ROWS * (1 - half)
    part = jnp.broadcast_to(window[:, start : start + width], (ROWS, width))
    return pltpu.roll(part, width - ROWS, axis=1, stride=1, stride_axis=0)[:, :queries]


def attention_forward_kernel(q_ref, k0, k1, k2, k3, v0, v1, v2, v3, w_ref, o_ref, l_ref, s_ref, p_ref):
    queries = q_ref[...]
    count = queries.shape[0]
    lanes = lax.broadcasted_iota(jnp.int32, queries.shape, 1)
    ks, vs = (k0, k1, k2, k3), (v0, v1, v2, v3)
    outs = []
    for head in range(2):
        own = (lanes < HEAD_DIM) if head == 0 else (lanes >= HEAD_DIM)
        q_head = jnp.where(own, queries, jnp.zeros_like(queries)) * jnp.asarray(1.0 / ROOT_SIZE, BF16)
        top = None
        for chunk in range(8):
            block, half = divmod(chunk, 2)
            rows = slice(half * ROWS, (half + 1) * ROWS)
            score = dot_nt(ks[block][rows, :], q_head)
            score = score + bias_rows(w_ref[head, block : block + 1, :], half, count)
            s_ref[chunk * ROWS : (chunk + 1) * ROWS, :] = score
            chunk_top = jnp.max(score, axis=0, keepdims=True)
            top = chunk_top if top is None else jnp.maximum(top, chunk_top)
        total = None
        for chunk in range(8):
            rows = slice(chunk * ROWS, (chunk + 1) * ROWS)
            expo = jnp.exp(s_ref[rows, :] - top)
            p_ref[rows, :] = expo.astype(BF16)
            part = jnp.sum(expo, axis=0, keepdims=True)
            total = part if total is None else total + part
        mixed = None
        for block in range(4):
            part = dot_tn(vs[block][...], p_ref[block * count : (block + 1) * count, :])
            mixed = part if mixed is None else mixed + part
        outs.append(mixed[head * HEAD_DIM : (head + 1) * HEAD_DIM, :] / total)
        l_ref[0, head : head + 1, :] = top + jnp.log(total)
    o_ref[...] = jnp.concatenate(outs, axis=0).T.astype(BF16)


def attention_forward(queries, keys, values, windows):
    rows, width = queries.shape
    pairs = HEADS // 2
    pair = 2 * HEAD_DIM
    chunk_spec = pl.BlockSpec((rows, pair), lambda g: (0, g))
    return pl.pallas_call(
        attention_forward_kernel,
        grid=(pairs,),
        in_specs=[chunk_spec] * 9 + [pl.BlockSpec((2,) + windows.shape[1:], lambda g: (g, 0, 0))],
        out_specs=[chunk_spec, pl.BlockSpec((1, 2, rows), lambda g: (g, 0, 0))],
        out_shape=[
            jax.ShapeDtypeStruct((rows, width), BF16),
            jax.ShapeDtypeStruct((pairs, 2, rows), F32),
        ],
        scratch_shapes=[pltpu.VMEM((4 * rows, rows), F32), pltpu.VMEM((4 * rows, rows), BF16)],
        cost_estimate=pl.CostEstimate(
            flops=16 * rows * rows * width, bytes_accessed=20 * rows * width, transcendentals=4 * rows * rows * HEADS
        ),
        name="attention_forward",
    )(queries, *keys, *values, windows)


def attention_backward_kernel(
    q_ref, g_ref, l_ref, k0, k1, k2, k3, v0, v1, v2, v3, w_ref,
    dq_ref, dk0, dk1, dk2, dk3, dv0, dv1, dv2, dv3, dw_ref, p_ref, d_ref, ds_ref, pb_ref,
):
    queries = q_ref[...]
    grads = g_ref[...]
    count = queries.shape[0]
    lanes = lax.broadcasted_iota(jnp.int32, queries.shape, 1)
    ks, vs = (k0, k1, k2, k3), (v0, v1, v2, v3)
    dks, dvs = (dk0, dk1, dk2, dk3), (dv0, dv1, dv2, dv3)
    key_sums, value_sums, query_parts = [None] * 4, [None] * 4, []
    for head in range(2):
        own = (lanes < HEAD_DIM) if head == 0 else (lanes >= HEAD_DIM)
        q_head = jnp.where(own, queries, jnp.zeros_like(queries)) * jnp.asarray(1.0 / ROOT_SIZE, BF16)
        g_head = jnp.where(own, grads, jnp.zeros_like(grads))
        level = l_ref[0, head : head + 1, :]
        row_dot = None
        for chunk in range(8):
            block, half = divmod(chunk, 2)
            rows = slice(half * ROWS, (half + 1) * ROWS)
            place = slice(chunk * ROWS, (chunk + 1) * ROWS)
            score = dot_nt(ks[block][rows, :], q_head)
            score = score + bias_rows(w_ref[head, block : block + 1, :], half, count)
            attention = jnp.exp(score - level)
            grad_attention = dot_nt(vs[block][rows, :], g_head)
            p_ref[place, :] = attention
            pb_ref[place, :] = attention.astype(BF16)
            d_ref[place, :] = grad_attention
            part = jnp.sum(attention * grad_attention, axis=0, keepdims=True)
            row_dot = part if row_dot is None else row_dot + part
        for chunk in range(8):
            block, half = divmod(chunk, 2)
            place = slice(chunk * ROWS, (chunk + 1) * ROWS)
            grad_score = (p_ref[place, :] * (d_ref[place, :] - row_dot)).astype(BF16)
            ds_ref[place, :] = grad_score
            sheared = jnp.concatenate([grad_score.astype(F32), jnp.zeros((ROWS, ROWS), F32)], axis=1)
            live = ROWS
            while live > 8:
                live = live // 2
                sheared = pltpu.roll(sheared[:live, :], live, axis=1) + sheared[live:, :]
            start = ROWS * (1 - half)
            if half == 0:
                dw_ref[head, block, :, 0:ROWS] = jnp.zeros((8, ROWS), F32)
                dw_ref[head, block, :, start : start + count + ROWS] = sheared
            else:
                dw_ref[head, block, :, start : start + count + ROWS] += sheared
        query_part = None
        for block in range(4):
            place = slice(block * count, (block + 1) * count)
            part = dot_tn(ks[block][...], ds_ref[place, :])
            query_part = part if query_part is None else query_part + part
            key_part = matmul(ds_ref[place, :], q_head)
            value_part = matmul(pb_ref[place, :], g_head)
            if head == 0:
                key_sums[block], value_sums[block] = key_part, value_part
            else:
                dks[block][...] = (key_sums[block] + key_part).astype(dks[block].dtype)
                dvs[block][...] = (value_sums[block] + value_part).astype(dvs[block].dtype)
        query_parts.append(query_part[head * HEAD_DIM : (head + 1) * HEAD_DIM, :])
    dq_ref[...] = (jnp.concatenate(query_parts, axis=0).T * (1.0 / ROOT_SIZE)).astype(BF16)


def attention_backward(queries, grads, levels, keys, values, windows):
    rows, width = queries.shape
    pairs = HEADS // 2
    pair = 2 * HEAD_DIM
    chunk_spec = pl.BlockSpec((rows, pair), lambda g: (0, g))
    span = windows.shape[-1]
    kinds = [BF16] + [F32, BF16, F32, BF16] * 2
    outs = pl.pallas_call(
        attention_backward_kernel,
        grid=(pairs,),
        in_specs=[chunk_spec] * 2
        + [pl.BlockSpec((1, 2, rows), lambda g: (g, 0, 0))]
        + [chunk_spec] * 8
        + [pl.BlockSpec((2,) + windows.shape[1:], lambda g: (g, 0, 0))],
        out_specs=[chunk_spec] * 9 + [pl.BlockSpec((2, 4, 8, span), lambda g: (g, 0, 0, 0))],
        out_shape=[jax.ShapeDtypeStruct((rows, width), kind) for kind in kinds]
        + [jax.ShapeDtypeStruct((HEADS, 4, 8, span), F32)],
        scratch_shapes=[
            pltpu.VMEM((4 * rows, rows), F32),
            pltpu.VMEM((4 * rows, rows), F32),
            pltpu.VMEM((4 * rows, rows), BF16),
            pltpu.VMEM((4 * rows, rows), BF16),
        ],
        cost_estimate=pl.CostEstimate(
            flops=40 * rows * rows * width, bytes_accessed=60 * rows * width, transcendentals=4 * rows * rows * HEADS
        ),
        name="attention_backward",
    )(queries, grads, levels, *keys, *values, windows)
    return outs[0], outs[1:5], outs[5:9], outs[9]


def fold_rows(sheared):
    span = sheared.shape[-1]
    total = 0.0
    for row in range(8):
        total = total + jnp.roll(sheared[..., row, :], 8 - row, axis=-1)
    return total


def section_swap(value):
    return lax.ppermute(value, SECTION, [(0, 1), (1, 0)])


def inner_swap(value):
    return shift_to(value, INNER, 1)


def outer_swap(value):
    return shift_to(value, OUTER, 1)


def rms_pull(values, gain, grad):
    scale = lax.rsqrt(jnp.mean(values * values, axis=-1, keepdims=True) + EPSILON)
    weighted = grad * gain
    lean = jnp.mean(weighted * values, axis=-1, keepdims=True)
    grad_values = scale * weighted - values * (scale * scale * scale * lean)
    grad_gain = jnp.sum(grad * values * scale, axis=0)
    return grad_values, grad_gain


def send_slots(rows, direction):
    count = lax.axis_size(EXPERT)
    parts = [rows[0]] + [shift_to(rows[k], EXPERT, direction * k) for k in range(1, count)]
    return jnp.concatenate(parts, axis=0)


def route_tables(route, capacity):
    tokens = route.shape[0]
    count = lax.axis_size(EXPERT)
    ahead = jnp.remainder(route - lax.axis_index(EXPERT) + count, count)
    onehot = (ahead[:, :, None] == jnp.arange(count, dtype=jnp.int32)).astype(F32)
    per_row = jnp.sum(onehot, axis=1)
    earlier = (jnp.arange(tokens)[:, None] > jnp.arange(tokens)[None, :]).astype(BF16)
    before = matmul(earlier, per_row.astype(BF16))
    slot_place = jnp.sum(before[:, None, :] * onehot, axis=2).astype(jnp.int32)
    target = ahead * capacity + slot_place
    slots = jnp.arange(count * capacity, dtype=jnp.int32)
    spots = (target[:, 0:1] == slots) | (target[:, 1:2] == slots)
    owner = jnp.remainder(slots // capacity + lax.axis_index(EXPERT), count)
    members = (owner[:, None] == jnp.arange(count, dtype=jnp.int32)).astype(F32)
    return spots, members


def forward(section_in, tables, weights, windows):
    spots, members = tables
    slot_table = spots.astype(BF16)
    slot_count = slot_table.shape[1]
    expert_count = lax.axis_size(EXPERT)
    inputs = section_in.astype(F32)
    width = inputs.shape[1]
    normed = rms_scale(inputs, weights["gain_first"]).astype(BF16)
    key_own = matmul(normed, weights["key"]).astype(BF16)
    value_own = matmul(normed, weights["value"]).astype(BF16)
    key_outer, value_outer = outer_swap(key_own), outer_swap(value_own)
    key_inner, value_inner = inner_swap(key_own), inner_swap(value_own)
    queries = matmul(normed, weights["query"]).astype(BF16)
    key_both, value_both = inner_swap(key_outer), inner_swap(value_outer)
    keys = (key_own, key_inner, key_outer, key_both)
    values = (value_own, value_inner, value_outer, value_both)
    attended, levels = attention_forward(queries, keys, values, windows)
    middle = inputs + matmul(attended, weights["output"])
    mixed_in = rms_scale(middle, weights["gain_second"]).astype(BF16)
    packed = dot_tn(slot_table, mixed_in).astype(BF16)
    arrived = send_slots(packed.reshape(expert_count, -1, width), 1)
    gates_all = softmax_rows(matmul(mixed_in, weights["router"]))
    spread = lax.dot_general(
        gates_all, members, (((1,), (1,)), ((), ())), precision=lax.Precision.HIGHEST, preferred_element_type=F32
    )
    combine = jnp.where(spots, spread, 0.0)
    combine_high = combine.astype(BF16)
    combine_low = (combine - combine_high.astype(F32)).astype(BF16)
    gate_part = matmul(arrived, weights["gate"])
    up_part = matmul(arrived, weights["up"])
    hidden = gated_gelu(gate_part, up_part).astype(BF16)
    produced = matmul(hidden, weights["down"]).astype(BF16)
    returned = send_slots(produced.reshape(expert_count, -1, width), -1)
    mixed_out = matmul(combine_high, returned) + matmul(combine_low, returned)
    result = (middle + mixed_out).astype(BF16)
    stored = (
        inputs, normed, queries, keys, values, attended, levels, middle, mixed_in, gates_all,
        arrived, gate_part, up_part, hidden, returned, combine_high, combine_low,
    )
    return result, stored


def backward(grad_rows, stored, tables, weights, windows, bucket_rows):
    spots, members = tables
    slot_table = spots.astype(BF16)
    (
        inputs, normed, queries, keys, values, attended, levels, middle, mixed_in, gates_all,
        arrived, gate_part, up_part, hidden, returned, combine_high, combine_low,
    ) = stored
    expert_count = lax.axis_size(EXPERT)
    width = inputs.shape[1]
    grad_out = grad_rows.astype(F32)
    grad_slots = (dot_tn(combine_high, grad_rows) + dot_tn(combine_low, grad_rows)).astype(BF16)
    received = send_slots(grad_slots.reshape(expert_count, -1, width), 1)
    products = jnp.where(spots, dot_nt(grad_rows, returned), 0.0)
    grad_gates = jnp.dot(products, members, precision=lax.Precision.HIGHEST, preferred_element_type=F32)
    grad_logits = gates_all * (grad_gates - jnp.sum(gates_all * grad_gates, axis=-1, keepdims=True))
    grad_logits = grad_logits.astype(BF16)
    term_router = dot_tn(mixed_in, grad_logits)

    grad_hidden = dot_nt(received, weights["down"])
    unused_value, pull_gelu = jax.vjp(gated_gelu, gate_part, up_part)
    grad_gate, grad_up = pull_gelu(grad_hidden)
    grad_gate = grad_gate.astype(BF16)
    grad_up = grad_up.astype(BF16)
    grad_arrived = (dot_nt(grad_gate, weights["gate"]) + dot_nt(grad_up, weights["up"])).astype(BF16)
    back_rows = send_slots(grad_arrived.reshape(expert_count, -1, width), -1)
    term_down = dot_tn(hidden, received).astype(BF16)
    term_gate = dot_tn(arrived, grad_gate).astype(BF16)
    term_up = dot_tn(arrived, grad_up).astype(BF16)

    grad_mixed = matmul(slot_table, back_rows) + dot_nt(grad_logits, weights["router"])
    grad_middle, term_second = rms_pull(middle, weights["gain_second"], grad_mixed)
    grad_middle = grad_middle + grad_out
    grad_branch = grad_middle.astype(BF16)
    grad_attended = dot_nt(grad_branch, weights["output"]).astype(BF16)
    term_output = dot_tn(attended, grad_branch).astype(BF16)
    grad_queries, key_parts, value_parts, sheared = attention_backward(
        queries, grad_attended, levels, keys, values, windows
    )

    def gather_parts(parts):
        own, inner, outer, both = parts
        passed = (outer + inner_swap(both).astype(F32)).astype(BF16)
        return own + inner_swap(inner).astype(F32) + outer_swap(passed).astype(F32)

    grad_keys = gather_parts(key_parts).astype(BF16)
    grad_values = gather_parts(value_parts).astype(BF16)
    grad_windows = fold_rows(sheared).reshape(HEADS, -1)
    term_position = lax.dot_general(
        grad_windows, bucket_rows.astype(F32), (((1,), (1,)), ((), ())),
        precision=lax.Precision.HIGHEST, preferred_element_type=F32,
    )
    term_query = dot_tn(normed, grad_queries).astype(BF16)
    term_key = dot_tn(normed, grad_keys).astype(BF16)
    term_value = dot_tn(normed, grad_values).astype(BF16)
    grad_normed = (
        dot_nt(grad_queries, weights["query"])
        + dot_nt(grad_keys, weights["key"])
        + dot_nt(grad_values, weights["value"])
    )
    grad_in, term_first = rms_pull(inputs, weights["gain_first"], grad_normed)
    grad_in = grad_in + grad_middle
    dense_terms = (term_query, term_key, term_value, term_output)
    small_terms = (term_router, term_first, term_second, term_position)
    expert_terms = (term_gate, term_up, term_down)
    return grad_in, dense_terms, small_terms, expert_terms


def pack_small(router, first, second, position, count):
    parts = [router.reshape(count, -1), first.reshape(count, -1), second.reshape(count, -1), position.reshape(count, -1)]
    flat = jnp.concatenate(parts, axis=1)
    return jnp.pad(flat, ((0, 0), (0, -flat.shape[1] % 1024)))


def unpack_small(flat, rows, experts, heads, buckets):
    sizes = [rows * experts, rows, rows, heads * buckets]
    starts = [sum(sizes[:k]) for k in range(5)]
    pieces = [flat[:, starts[k] : starts[k + 1]] for k in range(4)]
    return pieces[0].reshape(-1, experts), pieces[1].reshape(-1), pieces[2].reshape(-1), pieces[3].reshape(-1, buckets)


def shards(
    inputs,
    cotangent,
    routes,
    bucket_table,
    query_weight,
    key_weight,
    value_weight,
    output_weight,
    router_weight,
    attention_gain,
    mixture_gain,
    position_bias,
    expert_gate,
    expert_up,
    expert_down,
):
    micro_count = inputs.shape[0]
    tok_rows = inputs.shape[2]
    model_width = inputs.shape[3]
    expert_count = lax.axis_size(EXPERT)
    replica_count = lax.axis_size(OUTER) * lax.axis_size(INNER)
    assert micro_count == lax.axis_size(SECTION) == 2 and replica_count == 4
    capacity = max(2, 9 * tok_rows // (4 * expert_count))
    length = tok_rows * replica_count
    buckets = position_bias.shape[2]
    section_index = lax.axis_index(SECTION)
    replica_index = 2 * lax.axis_index(OUTER) + lax.axis_index(INNER)
    first_section = section_index == 0

    own_rows = lax.dynamic_index_in_dim(inputs[:, 0], section_index, 0, keepdims=False)
    own_cotangent = lax.dynamic_index_in_dim(cotangent[:, 0], section_index, 0, keepdims=False)
    layer_routes = routes[0, :, 0]
    route_kept = lax.dynamic_index_in_dim(layer_routes, section_index, 0, keepdims=False)
    route_given = lax.dynamic_index_in_dim(layer_routes, 1 - section_index, 0, keepdims=False)
    route_taken = section_swap(route_given)
    layer_route = (
        jnp.where(first_section, route_kept, route_taken),
        jnp.where(first_section, route_taken, route_kept),
    )

    dense_rows = query_weight.shape[1]
    dense_stack = jnp.stack([query_weight[0], key_weight[0], value_weight[0], output_weight[0]])
    dense_piece = lax.dynamic_index_in_dim(dense_stack, replica_index, 0, keepdims=False)
    dense_all = lax.all_gather(dense_piece, (SECTION, OUTER, INNER, EXPERT), axis=0, tiled=False)
    dense_all = dense_all.reshape(2, 4, model_width, model_width)
    heads_own = position_bias.shape[1]
    small_piece = pack_small(router_weight[0], attention_gain[0], mixture_gain[0], position_bias[0], 1)
    small_all = lax.all_gather(small_piece[0].reshape(-1, 128), (SECTION, EXPERT), axis=0, tiled=False)
    small_all = small_all.reshape(2, expert_count, -1)
    gate_all = lax.all_gather(expert_gate[0, 0], (SECTION,) + REPLICA, axis=0, tiled=False)
    up_all = lax.all_gather(expert_up[0, 0], (SECTION,) + REPLICA, axis=0, tiled=False)
    down_all = lax.all_gather(expert_down[0, 0], (SECTION,) + REPLICA, axis=0, tiled=False)
    hidden_width = expert_gate.shape[3]
    gate_all = gate_all.reshape(2, model_width, hidden_width)
    up_all = up_all.reshape(2, model_width, hidden_width)
    down_all = down_all.reshape(2, replica_count, hidden_width, -1)

    reversed_table = jnp.concatenate([jnp.full((1,), -1, jnp.int32), bucket_table[::-1]])
    bucket_onehot = (jnp.arange(buckets, dtype=jnp.int32)[:, None] == reversed_table[None, :]).astype(BF16)
    bucket_rows = jnp.concatenate(
        [
            lax.dynamic_slice(
                bucket_onehot,
                (0, (3 + replica_index - jnp.bitwise_xor(replica_index, ahead)) * tok_rows),
                (buckets, 2 * tok_rows),
            )
            for ahead in range(4)
        ],
        axis=1,
    )

    layers = []
    for layer in range(2):
        router, first, second, position = unpack_small(small_all[layer], dense_rows, expert_count, heads_own, buckets)
        weights = dict(
            query=dense_all[layer, 0],
            key=dense_all[layer, 1],
            value=dense_all[layer, 2],
            output=dense_all[layer, 3],
            router=router,
            gain_first=first.astype(F32),
            gain_second=second.astype(F32),
            gate=gate_all[layer],
            up=up_all[layer],
            down=down_all[layer].transpose(1, 0, 2).reshape(hidden_width, model_width),
        )
        windows = matmul(position, bucket_rows).reshape(HEADS, 4, 2 * tok_rows)
        layers.append((weights, windows, route_tables(layer_route[layer], capacity)))

    rows, outputs, kept = own_rows, [], []
    for weights, windows, tables in layers:
        rows, stored = forward(rows, tables, weights, windows)
        outputs.append(rows)
        kept.append(stored)

    grads, results = own_cotangent, [None, None]
    input_grads = [None, None]
    for layer in (1, 0):
        weights, windows, tables = layers[layer]
        grad_in, dense_terms, small_terms, expert_terms = backward(
            grads, kept[layer], tables, weights, windows, bucket_rows
        )
        grads = grad_in.astype(BF16)
        input_grads[layer] = (grad_in, grads)
        gate_share = lax.psum_scatter(expert_terms[0], REPLICA, scatter_dimension=0, tiled=True)
        up_share = lax.psum_scatter(expert_terms[1], REPLICA, scatter_dimension=0, tiled=True)
        down_share = lax.psum_scatter(expert_terms[2], REPLICA, scatter_dimension=1, tiled=True)
        dense = jnp.stack(dense_terms).reshape(4 * expert_count, dense_rows, model_width)
        dense_share = lax.psum_scatter(dense, REPLICA + (EXPERT,), scatter_dimension=0, tiled=False)
        small = pack_small(*small_terms, expert_count)
        results[layer] = ((gate_share, up_share, down_share, dense_share), small)

    def settle(layer_pair):
        zero, one = layer_pair
        from_zero = lax.ppermute(zero, SECTION, [(1, 0)])
        from_one = lax.ppermute(one, SECTION, [(0, 1)])
        own = jnp.where(first_section, zero, one).astype(F32)
        other = jnp.where(first_section, from_zero, from_one).astype(F32)
        return own + other

    final_gate, final_up, final_down, final_dense = (
        settle((results[0][0][k], results[1][0][k])) for k in range(4)
    )
    final_dense = lax.all_gather(final_dense.astype(BF16), REPLICA, axis=0, tiled=False).astype(F32)
    small_sum = lax.psum(
        jnp.stack([results[0][1], results[1][1]]).astype(BF16), (SECTION, EXPERT) + REPLICA
    ).astype(F32)
    small_own = lax.dynamic_slice(
        small_sum, (section_index, lax.axis_index(EXPERT), 0), (1, 1, small_sum.shape[2])
    )[0]
    final_router, final_first, final_second, final_position = unpack_small(
        small_own, dense_rows, expert_count, heads_own, buckets
    )

    def both_micros(kept_one, taken_one):
        return jnp.where(
            first_section, jnp.stack([kept_one, taken_one]), jnp.stack([taken_one, kept_one])
        )[None, :, None]

    output_taken = section_swap(jnp.where(first_section, outputs[1], outputs[0]))
    section_output = both_micros(jnp.where(first_section, outputs[0], outputs[1]), output_taken)
    grad_from_one = lax.ppermute(input_grads[1][1], SECTION, [(0, 1)])
    grad_from_zero = lax.ppermute(input_grads[0][1], SECTION, [(1, 0)])
    grad_taken = jnp.where(first_section, grad_from_zero, grad_from_one).astype(F32)
    grad_kept = jnp.where(first_section, input_grads[0][0], input_grads[1][0])
    input_gradient = both_micros(grad_kept, grad_taken)
    return (
        section_output,
        input_gradient,
        final_dense[0:1],
        final_dense[1:2],
        final_dense[2:3],
        final_dense[3:4],
        final_router[None],
        final_first[None],
        final_second[None],
        final_position[None],
        final_gate[None, None],
        final_up[None, None],
        final_down[None, None],
    )


def solution(mesh):
    sections, experts, replicas = (mesh.shape[name] for name in ("section", "expert", "replica"))
    fine = Mesh(
        mesh.devices.reshape(sections, experts, replicas // 2, 2), (SECTION, EXPERT, OUTER, INNER)
    )
    rep = REPLICA
    in_specs = (
        P(None, "expert", rep, None),
        P(None, "expert", rep, None),
        P("section", None, "expert", rep, None),
        P(),
        P("section", "expert", None),
        P("section", "expert", None),
        P("section", "expert", None),
        P("section", "expert", None),
        P("section", "expert", None),
        P("section", "expert"),
        P("section", "expert"),
        P("section", "expert", None),
        P("section", "expert", rep, None),
        P("section", "expert", rep, None),
        P("section", "expert", None, rep),
    )
    out_specs = (
        P("section", None, "expert", rep, None),
        P("section", None, "expert", rep, None),
        P("section", "expert", None),
        P("section", "expert", None),
        P("section", "expert", None),
        P("section", "expert", None),
        P("section", "expert", None),
        P("section", "expert"),
        P("section", "expert"),
        P("section", "expert", None),
        P("section", "expert", rep, None),
        P("section", "expert", rep, None),
        P("section", "expert", None, rep),
    )
    return jax.shard_map(shards, mesh=fine, in_specs=in_specs, out_specs=out_specs, check_vma=False)
```

```python
import functools
import math

import jax
import jax.numpy as jnp
from jax import lax
from jax.experimental import pallas as pl
from jax.experimental.pallas import tpu as pltpu
from jax.sharding import Mesh
from jax.sharding import PartitionSpec as P

HEADS = 16
HEAD_DIM = 64
EPSILON = 1e-06
ROOT_SIZE = math.sqrt(HEAD_DIM)

SECTION = "section"
EXPERT = "expert"
OUTER = "outer"
INNER = "inner"
REPLICA = (OUTER, INNER)

BF16 = jnp.bfloat16
F32 = jnp.float32
ROWS = 128


def matmul(left, right):
    return jnp.dot(left, right, preferred_element_type=F32)


def dot_nt(left, right):
    return lax.dot_general(left, right, (((1,), (1,)), ((), ())), preferred_element_type=F32)


def dot_tn(left, right):
    return lax.dot_general(left, right, (((0,), (0,)), ((), ())), preferred_element_type=F32)


def rms_scale(values, gain):
    return values * lax.rsqrt(jnp.mean(values * values, axis=-1, keepdims=True) + EPSILON) * gain


def softmax_rows(scores):
    row_top = jnp.max(scores, axis=-1, keepdims=True)
    expos = jnp.exp(scores - row_top)
    return expos / jnp.sum(expos, axis=-1, keepdims=True)


def gated_gelu(gate_part, up_part):
    return jax.nn.gelu(gate_part, approximate=True) * up_part


def shift_to(value, axis, steps):
    count = lax.axis_size(axis)
    return lax.ppermute(value, axis, [(source, (source + steps) % count) for source in range(count)])


def bias_rows(window, half, queries):
    width = queries + ROWS
    start = ROWS * (1 - half)
    part = jnp.broadcast_to(window[:, start : start + width], (ROWS, width))
    return pltpu.roll(part, width - ROWS, axis=1, stride=1, stride_axis=0)[:, :queries]


def attention_forward_kernel(q_ref, k0, k1, k2, k3, v0, v1, v2, v3, w_ref, o_ref, x_ref, l_ref, s_ref, p_ref):
    queries = q_ref[...]
    count = queries.shape[0]
    lanes = lax.broadcasted_iota(jnp.int32, queries.shape, 1)
    ks, vs = (k0, k1, k2, k3), (v0, v1, v2, v3)
    outs = []
    for head in range(2):
        own = (lanes < HEAD_DIM) if head == 0 else (lanes >= HEAD_DIM)
        q_head = jnp.where(own, queries, jnp.zeros_like(queries)) * jnp.asarray(1.0 / ROOT_SIZE, BF16)
        top = None
        for chunk in range(8):
            block, half = divmod(chunk, 2)
            rows = slice(half * ROWS, (half + 1) * ROWS)
            score = dot_nt(ks[block][rows, :], q_head)
            score = score + bias_rows(w_ref[head, block : block + 1, :], half, count)
            s_ref[chunk * ROWS : (chunk + 1) * ROWS, :] = score
            chunk_top = jnp.max(score, axis=0, keepdims=True)
            top = chunk_top if top is None else jnp.maximum(top, chunk_top)
        total = None
        for chunk in range(8):
            rows = slice(chunk * ROWS, (chunk + 1) * ROWS)
            expo = jnp.exp(s_ref[rows, :] - top)
            p_ref[rows, :] = expo.astype(BF16)
            part = jnp.sum(expo, axis=0, keepdims=True)
            total = part if total is None else total + part
        mixed = None
        for block in range(4):
            part = dot_tn(vs[block][...], p_ref[block * count : (block + 1) * count, :])
            mixed = part if mixed is None else mixed + part
        outs.append(mixed[head * HEAD_DIM : (head + 1) * HEAD_DIM, :] / total)
        l_ref[0, head : head + 1, :] = top + jnp.log(total)
    mixed_rows = jnp.concatenate(outs, axis=0).T
    o_ref[...] = mixed_rows.astype(BF16)
    x_ref[...] = mixed_rows


def attention_forward(queries, pairs_kv, windows):
    rows, width = queries.shape
    pairs = HEADS // 2
    pair = 2 * HEAD_DIM
    chunk_spec = pl.BlockSpec((rows, pair), lambda g: (0, g))
    value_spec = pl.BlockSpec((rows, pair), lambda g: (0, g + HEADS // 2))
    return pl.pallas_call(
        attention_forward_kernel,
        grid=(pairs,),
        in_specs=[chunk_spec] * 5
        + [value_spec] * 4
        + [pl.BlockSpec((2,) + windows.shape[1:], lambda g: (g, 0, 0))],
        out_specs=[chunk_spec, chunk_spec, pl.BlockSpec((1, 2, rows), lambda g: (g, 0, 0))],
        out_shape=[
            jax.ShapeDtypeStruct((rows, width), BF16),
            jax.ShapeDtypeStruct((rows, width), F32),
            jax.ShapeDtypeStruct((pairs, 2, rows), F32),
        ],
        scratch_shapes=[pltpu.VMEM((4 * rows, rows), F32), pltpu.VMEM((4 * rows, rows), BF16)],
        cost_estimate=pl.CostEstimate(
            flops=16 * rows * rows * width, bytes_accessed=20 * rows * width, transcendentals=4 * rows * rows * HEADS
        ),
        name="attention_forward",
    )(queries, *pairs_kv, *pairs_kv, windows)


def attention_backward_kernel(
    q_ref, g_ref, o_ref, l_ref, k0, k1, v0, v1, w_ref, *rest, given
):
    given_ref, rest = (rest[0], rest[1:]) if given else (None, rest)
    dq_ref, dkv0, dkv1, dw_ref, ds_ref, pb_ref, w8_ref = rest
    queries = q_ref[...]
    grads = g_ref[...]
    count = queries.shape[0]
    lanes = lax.broadcasted_iota(jnp.int32, queries.shape, 1)
    ks, vs, dkvs = (k0, k1), (v0, v1), (dkv0, dkv1)
    products = (grads.astype(F32) * o_ref[...]).T
    key_sums, value_sums, query_parts = [None] * 2, [None] * 2, []
    for head in range(2):
        own = (lanes < HEAD_DIM) if head == 0 else (lanes >= HEAD_DIM)
        place_head = slice(head * HEAD_DIM, (head + 1) * HEAD_DIM)
        q_head = jnp.where(own, queries, jnp.zeros_like(queries)) * jnp.asarray(1.0 / ROOT_SIZE, BF16)
        g_head = jnp.where(own, grads, jnp.zeros_like(grads))
        level = l_ref[0, head : head + 1, :]
        row_dot = jnp.sum(products[place_head, :], axis=0, keepdims=True)
        for chunk in range(4):
            block, half = divmod(chunk, 2)
            rows = slice(half * ROWS, (half + 1) * ROWS)
            place = slice(chunk * ROWS, (chunk + 1) * ROWS)
            score = dot_nt(ks[block][rows, :], q_head)
            score = score + bias_rows(w_ref[head, block : block + 1, :], half, count)
            attention = jnp.exp(score - level)
            pb_ref[place, :] = attention.astype(BF16)
            grad_attention = dot_nt(vs[block][rows, :], g_head)
            grad_score = (attention * (grad_attention - row_dot)).astype(BF16)
            ds_ref[place, :] = grad_score
            sheared = jnp.concatenate([grad_score.astype(F32), jnp.zeros((ROWS, ROWS), F32)], axis=1)
            live = ROWS
            while live > 8:
                live = live // 2
                sheared = pltpu.roll(sheared[:live, :], live, axis=1) + sheared[live:, :]
            start = ROWS * (1 - half)
            if half == 0:
                w8_ref[block, :, 0:ROWS] = jnp.zeros((8, ROWS), F32)
                w8_ref[block, :, start : start + count + ROWS] = sheared
            else:
                w8_ref[block, :, start : start + count + ROWS] += sheared
        query_part = None
        for block in range(2):
            place = slice(block * count, (block + 1) * count)
            part = dot_tn(ks[block][...], ds_ref[place, :])
            query_part = part if query_part is None else query_part + part
            key_part = matmul(ds_ref[place, :], q_head)
            value_part = matmul(pb_ref[place, :], g_head)
            if head == 0:
                key_sums[block], value_sums[block] = key_part, value_part
            else:
                dkvs[block][0] = (key_sums[block] + key_part).astype(dkvs[block].dtype)
                dkvs[block][1] = (value_sums[block] + value_part).astype(dkvs[block].dtype)
        query_parts.append(query_part[place_head, :])
        for block in range(2):
            folded = pltpu.roll(w8_ref[block], 1, axis=1)
            rows8 = lax.broadcasted_iota(jnp.int32, folded.shape, 0)
            for bit in (1, 2, 4):
                folded = jnp.where(jnp.bitwise_and(rows8, bit) == 0, pltpu.roll(folded, bit, axis=1), folded)
            dw_ref[head, block : block + 1, :] = jnp.sum(folded, axis=0, keepdims=True)
    grad_queries = jnp.concatenate(query_parts, axis=0).T * (1.0 / ROOT_SIZE)
    if given:
        grad_queries = grad_queries + given_ref[...]
    dq_ref[...] = grad_queries.astype(dq_ref.dtype)


def attention_backward(queries, grads, attended, levels, pairs_kv, windows, given=None):
    rows, width = queries.shape
    pairs = HEADS // 2
    pair = 2 * HEAD_DIM
    chunk_spec = pl.BlockSpec((rows, pair), lambda g: (0, g))
    value_spec = pl.BlockSpec((rows, pair), lambda g: (0, g + HEADS // 2))
    window_spec = pl.BlockSpec((2,) + windows.shape[1:], lambda g: (g, 0, 0))
    span = windows.shape[-1]
    extra = [] if given is None else [given]
    return pl.pallas_call(
        functools.partial(attention_backward_kernel, given=given is not None),
        grid=(pairs,),
        in_specs=[chunk_spec] * 3
        + [pl.BlockSpec((1, 2, rows), lambda g: (g, 0, 0))]
        + [chunk_spec] * 2
        + [value_spec] * 2
        + [window_spec]
        + [chunk_spec] * len(extra),
        out_specs=[chunk_spec]
        + [pl.BlockSpec((2, rows, pair), lambda g: (0, 0, g))] * 2
        + [pl.BlockSpec((2, 2, span), lambda g: (g, 0, 0))],
        out_shape=[
            jax.ShapeDtypeStruct((rows, width), F32 if given is None else BF16),
            jax.ShapeDtypeStruct((2, rows, width), F32),
            jax.ShapeDtypeStruct((2, rows, width), BF16),
            jax.ShapeDtypeStruct((HEADS, 2, span), F32),
        ],
        scratch_shapes=[
            pltpu.VMEM((2 * rows, rows), BF16),
            pltpu.VMEM((2 * rows, rows), BF16),
            pltpu.VMEM((2, 8, span), F32),
        ],
        cost_estimate=pl.CostEstimate(
            flops=20 * rows * rows * width, bytes_accessed=36 * rows * width, transcendentals=2 * rows * rows * HEADS
        ),
        name="attention_backward",
    )(queries, grads, attended, levels, *pairs_kv, *pairs_kv, windows, *extra)


def section_swap(value):
    return lax.ppermute(value, SECTION, [(0, 1), (1, 0)])


def inner_swap(value):
    return shift_to(value, INNER, 1)


def outer_swap(value):
    return shift_to(value, OUTER, 1)


def rms_pull(values, gain, grad):
    scale = lax.rsqrt(jnp.mean(values * values, axis=-1, keepdims=True) + EPSILON)
    weighted = grad * gain
    lean = jnp.mean(weighted * values, axis=-1, keepdims=True)
    grad_values = scale * weighted - values * (scale * scale * scale * lean)
    grad_gain = jnp.sum(grad * values * scale, axis=0)
    return grad_values, grad_gain


def send_slots(rows, direction):
    count = lax.axis_size(EXPERT)
    parts = [rows[0]] + [shift_to(rows[k], EXPERT, direction * k) for k in range(1, count)]
    return jnp.concatenate(parts, axis=0)


def route_tables(route, capacity):
    tokens = route.shape[0]
    count = lax.axis_size(EXPERT)
    ahead = jnp.remainder(route - lax.axis_index(EXPERT) + count, count)
    onehot = (ahead[:, :, None] == jnp.arange(count, dtype=jnp.int32)).astype(F32)
    per_row = jnp.sum(onehot, axis=1)
    earlier = (jnp.arange(tokens)[:, None] > jnp.arange(tokens)[None, :]).astype(BF16)
    before = matmul(earlier, per_row.astype(BF16))
    slot_place = jnp.sum(before[:, None, :] * onehot, axis=2).astype(jnp.int32)
    target = ahead * capacity + slot_place
    slots = jnp.arange(count * capacity, dtype=jnp.int32)
    spots = (target[:, 0:1] == slots) | (target[:, 1:2] == slots)
    owner = jnp.remainder(slots // capacity + lax.axis_index(EXPERT), count)
    members = (owner[:, None] == jnp.arange(count, dtype=jnp.int32)).astype(F32)
    return spots, members


def forward(section_in, tables, weights, windows, started):
    spots, members = tables
    slot_table = spots.astype(BF16)
    slot_count = slot_table.shape[1]
    expert_count = lax.axis_size(EXPERT)
    inputs = section_in.astype(F32)
    width = inputs.shape[1]
    if started is None:
        normed = rms_scale(inputs, weights["gain_first"]).astype(BF16)
        pair_own = matmul(normed, weights["pair"]).astype(BF16)
        pair_outer = outer_swap(pair_own)
    else:
        normed, pair_own, pair_outer = started
    pair_inner = inner_swap(pair_own)
    queries = matmul(normed, weights["query"]).astype(BF16)
    pair_both = inner_swap(pair_outer)
    pairs_kv = (pair_own, pair_inner, pair_outer, pair_both)
    attended, attended_full, levels = attention_forward(queries, pairs_kv, windows)
    middle = inputs + matmul(attended, weights["output"])
    mixed_in = rms_scale(middle, weights["gain_second"]).astype(BF16)
    packed = dot_tn(slot_table, mixed_in).astype(BF16)
    arrived = send_slots(packed.reshape(expert_count, -1, width), 1)
    gates_all = softmax_rows(matmul(mixed_in, weights["router"]))
    spread = lax.dot_general(
        gates_all, members, (((1,), (1,)), ((), ())), precision=lax.Precision.HIGHEST, preferred_element_type=F32
    )
    combine = jnp.where(spots, spread, 0.0)
    combine_high = combine.astype(BF16)
    combine_low = (combine - combine_high.astype(F32)).astype(BF16)
    gate_part = matmul(arrived, weights["gate"])
    up_part = matmul(arrived, weights["up"])
    hidden = gated_gelu(gate_part, up_part).astype(BF16)
    produced = dot_nt(hidden, weights["down"]).astype(BF16)
    returned = send_slots(produced.reshape(expert_count, -1, width), -1)
    mixed_out = matmul(combine_high, returned) + matmul(combine_low, returned)
    result = (middle + mixed_out).astype(BF16)
    stored = (
        inputs, normed, queries, pairs_kv, attended, attended_full, levels, middle, mixed_in, gates_all,
        arrived, gate_part, up_part, hidden, returned, combine_high, combine_low,
    )
    return result, stored


def backward(grad_rows, stored, tables, weights, windows, bucket_rows, offload, waited):
    spots, members = tables
    slot_table = spots.astype(BF16)
    (
        inputs, normed, queries, pairs_kv, attended, attended_full, levels, middle, mixed_in, gates_all,
        arrived, gate_part, up_part, hidden, returned, combine_high, combine_low,
    ) = stored
    expert_count = lax.axis_size(EXPERT)
    width = inputs.shape[1]
    grad_out = grad_rows.astype(F32)
    grad_slots = (dot_tn(combine_high, grad_rows) + dot_tn(combine_low, grad_rows)).astype(BF16)
    if offload:
        grad_slots, arrived = lax.optimization_barrier((grad_slots, arrived))
    received = send_slots(grad_slots.reshape(expert_count, -1, width), 1)
    received, waited[0] = lax.optimization_barrier((received, waited[0]))
    products = jnp.where(spots, dot_nt(grad_rows, returned), 0.0)
    grad_gates = jnp.dot(products, members, precision=lax.Precision.HIGHEST, preferred_element_type=F32)
    grad_logits = gates_all * (grad_gates - jnp.sum(gates_all * grad_gates, axis=-1, keepdims=True))
    grad_logits = grad_logits.astype(BF16)
    term_router = dot_tn(mixed_in, grad_logits)

    def for_inner(left, right):
        return dot_tn(inner_columns(left, 1), right).astype(BF16)

    def from_inner(term):
        return inner_swap(term).reshape(2, -1, term.shape[1])

    def for_outer(left, right, taken):
        return plus(dot_tn(replica_columns(left, 1), right), take(taken, 1 - lax.axis_index(OUTER), 0))

    down_given, received = lax.optimization_barrier((for_inner(received, hidden), received))
    down_inner = from_inner(down_given)
    grad_hidden = matmul(received, weights["down"])
    unused_value, pull_gelu = jax.vjp(gated_gelu, gate_part, up_part)
    grad_gate, grad_up = pull_gelu(grad_hidden)
    grad_gate, grad_up, down_inner = lax.optimization_barrier(
        (grad_gate.astype(BF16), grad_up.astype(BF16), down_inner)
    )
    grad_gate, grad_up, down_given = lax.optimization_barrier(
        (grad_gate, grad_up, for_outer(received, hidden, down_inner))
    )
    down_outer = outer_swap(down_given)
    gate_given, up_given, grad_gate, grad_up = lax.optimization_barrier(
        (for_inner(arrived, grad_gate), for_inner(arrived, grad_up), grad_gate, grad_up)
    )
    gate_inner, up_inner = from_inner(gate_given), from_inner(up_given)
    grad_arrived = (dot_nt(grad_gate, weights["gate"]) + dot_nt(grad_up, weights["up"])).astype(BF16)
    grad_arrived, gate_inner, up_inner = lax.optimization_barrier((grad_arrived, gate_inner, up_inner))
    back_rows = send_slots(grad_arrived.reshape(expert_count, -1, width), -1)
    gate_given = for_outer(arrived, grad_gate, gate_inner)
    up_given = for_outer(arrived, grad_up, up_inner)
    back_rows, gate_given, up_given, down_outer, waited[1] = lax.optimization_barrier(
        (back_rows, gate_given, up_given, down_outer, waited[1])
    )
    gate_outer = outer_swap(gate_given)

    grad_mixed = matmul(slot_table, back_rows) + dot_nt(grad_logits, weights["router"])
    grad_middle, term_second = rms_pull(middle, weights["gain_second"], grad_mixed)
    grad_middle = grad_middle + grad_out
    grad_branch = grad_middle.astype(BF16)
    grad_attended = dot_nt(grad_branch, weights["output"]).astype(BF16)
    term_output = dot_tn(attended, grad_branch).astype(BF16)
    grad_attended, gate_outer, waited[2] = lax.optimization_barrier((grad_attended, gate_outer, waited[2]))
    up_outer = outer_swap(up_given)
    grad_part, outer, both, windows_far = attention_backward(
        queries, grad_attended, attended_full, levels, pairs_kv[2:], windows[:, 2:]
    )
    far_taken = inner_swap(both)
    grad_part, far_taken, up_outer, waited[3] = lax.optimization_barrier((grad_part, far_taken, up_outer, waited[3]))
    passed = plus(outer, far_taken)
    passed, grad_part = lax.optimization_barrier((passed, grad_part))
    outer_sum = outer_swap(passed)
    grad_queries, own, inner, windows_near = attention_backward(
        queries, grad_attended, attended_full, levels, pairs_kv[:2], windows[:, :2], grad_part
    )
    grad_queries, own, inner, outer_sum, waited[4] = lax.optimization_barrier(
        (grad_queries, own, inner, outer_sum, waited[4])
    )
    grad_windows = jnp.concatenate([windows_near, windows_far], axis=1)
    near_sum = own + inner_swap(inner).astype(F32)
    grad_windows = grad_windows.reshape(HEADS, -1)
    term_position = lax.dot_general(
        grad_windows, bucket_rows.astype(F32), (((1,), (1,)), ((), ())),
        precision=lax.Precision.HIGHEST, preferred_element_type=F32,
    )
    grad_normed = dot_nt(grad_queries, weights["query"])
    small_early = (term_router, term_second, term_position)
    if offload:
        term_query = dot_tn(normed, grad_queries).astype(BF16)
        term_output = dot_tn(attended, grad_branch).astype(BF16)
        near_sum, grad_normed, term_query, term_output, small_early = lax.optimization_barrier(
            (near_sum, grad_normed, term_query, term_output, small_early)
        )
    else:
        even = lax.axis_index(INNER) == 0
        lefts, rights = (attended, normed), (grad_branch, grad_queries)
        first_fold = fold_dense(
            (jnp.where(even, *lefts), jnp.where(even, *rights)),
            (jnp.where(even, *lefts[::-1]), jnp.where(even, *rights[::-1])),
        )
        near_sum, grad_normed, first_fold[0], small_early, waited[5] = lax.optimization_barrier(
            (near_sum, grad_normed, first_fold[0], small_early, waited[5])
        )
    grad_pair = (near_sum + outer_sum.astype(F32)).astype(BF16)
    if offload:
        grad_normed = grad_normed + dot_nt(grad_pair[0], weights["key"]) + dot_nt(grad_pair[1], weights["value"])
    else:
        index = lax.axis_index(INNER)
        second_fold = fold_dense((normed, take(grad_pair, index, 0)), (normed, take(grad_pair, 1 - index, 0)))
        second_fold[0], grad_pair = lax.optimization_barrier((second_fold[0], grad_pair))
        grad_normed = grad_normed + dot_nt(grad_pair[0], weights["key"]) + dot_nt(grad_pair[1], weights["value"])
    grad_in, term_first = rms_pull(inputs, weights["gain_first"], grad_normed)
    grad_in = grad_in + grad_middle
    small_terms = (small_early[0], term_first, small_early[1], small_early[2])
    pending = (
        (arrived, grad_gate, gate_inner, gate_outer),
        (arrived, grad_up, up_inner, up_outer),
        (received, hidden, down_inner, down_outer),
    )
    if offload:
        dense_terms = (
            term_output,
            term_query,
            dot_tn(normed, grad_pair[0]).astype(BF16),
            dot_tn(normed, grad_pair[1]).astype(BF16),
        )
    else:
        dense_terms = (first_fold, second_fold)
    return grad_in, dense_terms, small_terms, pending, waited


def finish_expert(pending):
    left, right, taken, last = pending
    return plus(dot_tn(replica_columns(left, 0), right) + take(taken, lax.axis_index(OUTER), 0).astype(F32), last)


def take(blocks, index, axis):
    return lax.dynamic_index_in_dim(blocks, index, axis, keepdims=False)


def plus(left, right):
    return (left.astype(F32) + right.astype(F32)).astype(BF16)


def pick_columns(values, index, size, count):
    parts = [
        lax.dynamic_slice_in_dim(values, start + index * size, size, 1)
        for start in range(0, values.shape[1], size * count)
    ]
    return jnp.concatenate(parts, axis=1)


def inner_columns(values, other):
    return pick_columns(values, jnp.bitwise_xor(lax.axis_index(INNER), other), values.shape[1] // 4, 2)


def replica_columns(values, other):
    width = values.shape[1] // 4
    place = 2 * jnp.bitwise_xor(lax.axis_index(OUTER), other) + lax.axis_index(INNER)
    return lax.dynamic_slice_in_dim(values, place * width, width, 1)


def fold_experts(blocks):
    count, index = lax.axis_size(EXPERT), lax.axis_index(EXPERT)
    total = take(blocks, index, 0).astype(F32)
    for ahead in range(1, count):
        given = take(blocks, jnp.remainder(index + ahead, count), 0)
        total = total + shift_to(given, EXPERT, ahead).astype(F32)
    return total


def fold_dense(own_pair, given_pair):
    given = dot_tn(*given_pair).astype(BF16)
    return [inner_swap(given), own_pair]


def finish_dense(fold):
    taken, (left, right) = fold
    outer_index, even = lax.axis_index(OUTER), lax.axis_index(INNER) == 0
    count = lax.axis_size(EXPERT)
    size = left.shape[1] // (2 * count)
    rows = taken.reshape(count, 2, -1, taken.shape[1])

    def part(index):
        term = dot_tn(pick_columns(left, index, size, 2), right)
        return term.reshape(count, -1, taken.shape[1]) + take(rows, index, 1).astype(F32)

    outer_taken = outer_swap(part(1 - outer_index).astype(BF16))
    total = fold_experts(plus(part(outer_index), outer_taken)).astype(BF16)
    total = plus(total, lax.ppermute(total, SECTION, [(1, 0)]))
    partner = outer_swap(total)
    lower = outer_index == 0
    own = jnp.concatenate([jnp.where(lower, total, partner), jnp.where(lower, partner, total)], axis=0)
    other = inner_swap(own)
    return jnp.where(even, own, other), jnp.where(even, other, own)


def fold_small(flat, source):
    flat = flat + inner_swap(flat)
    flat = flat + outer_swap(flat)
    flat = fold_experts(flat)
    return flat + lax.ppermute(flat, SECTION, [(source, 1 - source)])


def pack_small(router, first, second, position, count):
    parts = [router.reshape(count, -1), first.reshape(count, -1), second.reshape(count, -1), position.reshape(count, -1)]
    flat = jnp.concatenate(parts, axis=1)
    return jnp.pad(flat, ((0, 0), (0, -flat.shape[1] % 1024)))


def unpack_small(flat, rows, experts, heads, buckets):
    sizes = [rows * experts, rows, rows, heads * buckets]
    starts = [sum(sizes[:k]) for k in range(5)]
    pieces = [flat[:, starts[k] : starts[k + 1]] for k in range(4)]
    return pieces[0].reshape(-1, experts), pieces[1].reshape(-1), pieces[2].reshape(-1), pieces[3].reshape(-1, buckets)


def shards(
    inputs,
    cotangent,
    routes,
    bucket_table,
    query_weight,
    key_weight,
    value_weight,
    output_weight,
    router_weight,
    attention_gain,
    mixture_gain,
    position_bias,
    expert_gate,
    expert_up,
    expert_down,
):
    micro_count = inputs.shape[0]
    tok_rows = inputs.shape[2]
    model_width = inputs.shape[3]
    expert_count = lax.axis_size(EXPERT)
    replica_count = lax.axis_size(OUTER) * lax.axis_size(INNER)
    assert micro_count == lax.axis_size(SECTION) == 2 and replica_count == 4
    capacity = max(2, 9 * tok_rows // (4 * expert_count))
    length = tok_rows * replica_count
    buckets = position_bias.shape[2]
    section_index = lax.axis_index(SECTION)
    replica_index = 2 * lax.axis_index(OUTER) + lax.axis_index(INNER)
    first_section = section_index == 0

    own_rows = lax.dynamic_index_in_dim(inputs[:, 0], section_index, 0, keepdims=False)
    own_cotangent = lax.dynamic_index_in_dim(cotangent[:, 0], section_index, 0, keepdims=False)
    layer_routes = routes[0, :, 0]
    route_kept = lax.dynamic_index_in_dim(layer_routes, section_index, 0, keepdims=False)
    route_given = lax.dynamic_index_in_dim(layer_routes, 1 - section_index, 0, keepdims=False)
    route_taken = section_swap(route_given)
    layer_route = (
        jnp.where(first_section, route_kept, route_taken),
        jnp.where(first_section, route_taken, route_kept),
    )

    dense_rows = query_weight.shape[1]
    inner_index = lax.axis_index(INNER)
    expert_index = lax.axis_index(EXPERT)
    half_rows = dense_rows // 2

    def half_piece(*own_parts):
        return jnp.concatenate(
            [lax.dynamic_slice_in_dim(part, inner_index * half_rows, half_rows, 0) for part in own_parts], axis=1
        )

    def from_first(own):
        return jnp.where(first_section, own, lax.ppermute(own, SECTION, [(0, 1)]))

    def half_of(part, index):
        return lax.dynamic_slice_in_dim(part, index * (part.shape[0] // 2), part.shape[0] // 2, 0)

    def ring_gather(piece):
        whole = jnp.zeros((model_width, piece.shape[1]), BF16)
        for step in range(expert_count):
            start = jnp.remainder(expert_index - step + expert_count, expert_count) * dense_rows
            whole = lax.dynamic_update_slice(whole, piece, (start + inner_index * half_rows, 0))
            whole = lax.dynamic_update_slice(whole, inner_swap(piece), (start + (1 - inner_index) * half_rows, 0))
            if step + 1 < expert_count:
                piece = shift_to(piece, EXPERT, 1)
        return whole

    def half_of(part, index):
        return lax.dynamic_slice_in_dim(part, index * (part.shape[0] // 2), part.shape[0] // 2, 0)

    small_own = pack_small(router_weight[0], attention_gain[0], mixture_gain[0], position_bias[0], 1)[0]
    small_taken = section_swap(small_own)
    pair_piece = from_first(half_piece(key_weight[0], value_weight[0]))
    small_piece = jnp.where(
        first_section, jnp.stack([small_own, small_taken]), jnp.stack([small_taken, small_own])
    ).reshape(2, 1, -1)
    small_all = jnp.zeros((2, expert_count, small_piece.shape[2]), BF16)
    for step in range(expert_count):
        source = jnp.remainder(expert_index - step + expert_count, expert_count)
        small_all = lax.dynamic_update_slice(small_all, small_piece, (0, source, 0))
        if step + 1 < expert_count:
            small_piece = shift_to(small_piece, EXPERT, 1)

    second_own, pair_piece = lax.optimization_barrier(
        (half_piece(query_weight[0], output_weight[0]), pair_piece)
    )
    second_half = from_first(second_own)
    wide_own = (expert_gate[0, 0], expert_up[0, 0], expert_down[0, 0].T)
    wide_kept = jnp.concatenate([half_of(part, section_index) for part in wide_own], axis=1)
    wide_sent = jnp.concatenate([half_of(part, 1 - section_index) for part in wide_own], axis=1)
    wide_sent, second_half = lax.optimization_barrier((wide_sent, second_half))
    wide_taken = section_swap(wide_sent)
    first_pair = ring_gather(pair_piece)
    first_pair, small_all = lax.optimization_barrier((first_pair, small_all))
    small_parts = [
        unpack_small(small_all[layer], dense_rows, expert_count, position_bias.shape[1], position_bias.shape[2])
        for layer in range(2)
    ]
    normed = rms_scale(own_rows.astype(F32), small_parts[0][1].astype(F32)).astype(BF16)
    first_own = matmul(normed, first_pair).astype(BF16)
    second_half, first_own, wide_taken = lax.optimization_barrier((second_half, first_own, wide_taken))
    first_outer = outer_swap(first_own)
    second_whole = ring_gather(second_half)
    second_whole, first_outer = lax.optimization_barrier((second_whole, first_outer))
    first_query, first_output = second_whole[:, :model_width], second_whole[:, model_width:]

    eighth = dense_rows // 8

    def by_layer(kept_part, taken_part):
        return jnp.where(first_section, kept_part, taken_part), jnp.where(first_section, taken_part, kept_part)

    dense_axes = (EXPERT, SECTION) + REPLICA

    def eighths(*parts):
        kept_part = jnp.concatenate(
            [lax.dynamic_slice_in_dim(part, (4 * section_index + replica_index) * eighth, eighth, 0) for part in parts],
            axis=1,
        )
        sent_part = jnp.concatenate(
            [lax.dynamic_slice_in_dim(part, (4 * (1 - section_index) + replica_index) * eighth, eighth, 0) for part in parts],
            axis=1,
        )
        return kept_part, sent_part

    hidden_width = expert_gate.shape[3]
    rest_kept, rest_sent = eighths(key_weight[0], value_weight[0], query_weight[0], output_weight[0])
    rest_sent, first_own = lax.optimization_barrier((rest_sent, first_own))
    second_piece = by_layer(rest_kept, section_swap(rest_sent))[1]
    second_piece, first_query, first_own = lax.optimization_barrier((second_piece, first_query, first_own))
    heads_own = position_bias.shape[1]
    wide_pieces = by_layer(wide_kept, wide_taken)
    wide_all = []
    wide_all.append(lax.all_gather(wide_pieces[0], REPLICA + (SECTION,), axis=0, tiled=True))
    second_all = lax.all_gather(second_piece, dense_axes, axis=0, tiled=True)
    wide_all.append(lax.all_gather(wide_pieces[1], REPLICA + (SECTION,), axis=0, tiled=True))
    dense_all = (
        (first_pair, first_query, first_output),
        tuple(second_all[:, a * model_width : z * model_width] for a, z in ((0, 2), (2, 3), (3, 4))),
    )

    reversed_table = jnp.concatenate([jnp.full((1,), -1, jnp.int32), bucket_table[::-1]])
    bucket_onehot = (jnp.arange(buckets, dtype=jnp.int32)[:, None] == reversed_table[None, :]).astype(BF16)
    bucket_rows = jnp.concatenate(
        [
            lax.dynamic_slice(
                bucket_onehot,
                (0, (3 + replica_index - jnp.bitwise_xor(replica_index, ahead)) * tok_rows),
                (buckets, 2 * tok_rows),
            )
            for ahead in range(4)
        ],
        axis=1,
    )

    layers = []
    for layer in range(2):
        router, first, second, position = small_parts[layer]
        weights = dict(
            pair=dense_all[layer][0],
            key=dense_all[layer][0][:, :model_width],
            value=dense_all[layer][0][:, model_width:],
            query=dense_all[layer][1],
            output=dense_all[layer][2],
            router=router,
            gain_first=first.astype(F32),
            gain_second=second.astype(F32),
            gate=wide_all[layer][:, :hidden_width],
            up=wide_all[layer][:, hidden_width : 2 * hidden_width],
            down=wide_all[layer][:, 2 * hidden_width :],
        )
        windows = matmul(position, bucket_rows).reshape(HEADS, 4, 2 * tok_rows)
        layers.append((weights, windows, route_tables(layer_route[layer], capacity)))

    rows, outputs, kept = own_rows, [], []
    for weights, windows, tables in layers:
        rows, stored = forward(rows, tables, weights, windows, (normed, first_own, first_outer) if not kept else None)
        outputs.append(rows)
        kept.append(stored)

    weights, windows, tables = layers[1]
    grad_in_one, dense_terms, small_one, pending, waited = backward(
        own_cotangent, kept[1], tables, weights, windows, bucket_rows, True, [()] * 6
    )
    grads = grad_in_one.astype(BF16)
    small_one = pack_small(*small_one, expert_count).astype(BF16).reshape(1, expert_count, -1, model_width)
    small_one = jnp.pad(small_one, ((0, 3), (0, 0), (0, -small_one.shape[2] % 16), (0, 0)))
    dense = jnp.stack(dense_terms).reshape(4, expert_count, dense_rows, model_width)
    dense = jnp.concatenate([dense, small_one], axis=2).reshape(4 * expert_count, -1, model_width)
    grads, dense = lax.optimization_barrier((grads, dense))
    dense_share = lax.psum_scatter(dense, REPLICA + (EXPERT,), scatter_dimension=0, tiled=False)
    shares_one = [finish_expert(part) for part in pending]
    hops_one = [lax.ppermute(share, SECTION, [(0, 1)]) for share in shares_one]
    grad_from_one = lax.ppermute(grads, SECTION, [(0, 1)])

    weights, windows, tables = layers[0]
    waited = [tuple(shares_one), hops_one[2], grad_from_one, hops_one[0], (), hops_one[1]]
    grad_in_zero, folds_zero, small_zero, pending, waited = backward(
        grads, kept[0], tables, weights, windows, bucket_rows, False, waited
    )
    shares_one, hop_two, grad_from_one, hop_zero, unused, hop_one = waited
    hops_one = (hop_zero, hop_one, hop_two)
    shares_zero = [finish_expert(part) for part in pending]
    hops_zero = [lax.ppermute(share, SECTION, [(1, 0)]) for share in shares_zero]

    final_gate, final_up, final_down = (
        jnp.where(first_section, zero, one).astype(F32) + jnp.where(first_section, zero_hop, one_hop).astype(F32)
        for zero, zero_hop, one, one_hop in zip(shares_zero, hops_zero, shares_one, hops_one)
    )
    dense_share, grad_in_zero = lax.optimization_barrier((dense_share, grad_in_zero))
    dense_share = plus(dense_share, lax.ppermute(dense_share, SECTION, [(0, 1)]))
    dense_one = lax.all_gather(dense_share, REPLICA, axis=0, tiled=False)
    dense_zero = finish_dense(folds_zero[0]) + finish_dense(folds_zero[1])
    final_output, final_query, final_key, final_value = (
        jnp.where(first_section, dense_zero[k], dense_one[k, :dense_rows]).astype(F32) for k in range(4)
    )
    small_zero = fold_small(pack_small(*small_zero, expert_count), 1)
    small_one = dense_one[0, dense_rows:].reshape(-1)[: small_zero.shape[0]].astype(F32)
    final_router, final_first, final_second, final_position = unpack_small(
        jnp.where(first_section, small_zero, small_one).reshape(1, -1), dense_rows, expert_count, heads_own, buckets
    )

    def both_micros(kept_one, taken_one):
        return jnp.where(
            first_section, jnp.stack([kept_one, taken_one]), jnp.stack([taken_one, kept_one])
        )[None, :, None]

    output_taken = section_swap(jnp.where(first_section, outputs[1], outputs[0]))
    section_output = both_micros(jnp.where(first_section, outputs[0], outputs[1]), output_taken)
    grad_from_zero = lax.ppermute(grad_in_zero.astype(BF16), SECTION, [(1, 0)])
    grad_taken = jnp.where(first_section, grad_from_zero, grad_from_one).astype(F32)
    grad_kept = jnp.where(first_section, grad_in_zero, grad_in_one)
    input_gradient = both_micros(grad_kept, grad_taken)
    return (
        section_output,
        input_gradient,
        final_query[None],
        final_key[None],
        final_value[None],
        final_output[None],
        final_router[None],
        final_first[None],
        final_second[None],
        final_position[None],
        final_gate[None, None],
        final_up[None, None],
        final_down.T[None, None],
    )


def solution(mesh):
    sections, experts, replicas = (mesh.shape[name] for name in ("section", "expert", "replica"))
    fine = Mesh(
        mesh.devices.reshape(sections, experts, replicas // 2, 2), (SECTION, EXPERT, OUTER, INNER)
    )
    rep = REPLICA
    in_specs = (
        P(None, "expert", rep, None),
        P(None, "expert", rep, None),
        P("section", None, "expert", rep, None),
        P(),
        P("section", "expert", None),
        P("section", "expert", None),
        P("section", "expert", None),
        P("section", "expert", None),
        P("section", "expert", None),
        P("section", "expert"),
        P("section", "expert"),
        P("section", "expert", None),
        P("section", "expert", rep, None),
        P("section", "expert", rep, None),
        P("section", "expert", None, rep),
    )
    out_specs = (
        P("section", None, "expert", rep, None),
        P("section", None, "expert", rep, None),
        P("section", "expert", None),
        P("section", "expert", None),
        P("section", "expert", None),
        P("section", "expert", None),
        P("section", "expert", None),
        P("section", "expert"),
        P("section", "expert"),
        P("section", "expert", None),
        P("section", "expert", rep, None),
        P("section", "expert", rep, None),
        P("section", "expert", None, rep),
    )
    return jax.shard_map(shards, mesh=fine, in_specs=in_specs, out_specs=out_specs, check_vma=False)
```

```python
import functools
import math

import jax
import jax.numpy as jnp
from jax import lax
from jax.experimental import pallas as pl
from jax.experimental.pallas import tpu as pltpu
from jax.sharding import Mesh
from jax.sharding import PartitionSpec as P

HEADS = 16
HEAD_DIM = 64
EPSILON = 1e-06
ROOT_SIZE = math.sqrt(HEAD_DIM)

SECTION = "section"
EXPERT = "expert"
OUTER = "outer"
INNER = "inner"
REPLICA = (OUTER, INNER)

BF16 = jnp.bfloat16
F32 = jnp.float32
ROWS = 128


def matmul(left, right):
    return jnp.dot(left, right, preferred_element_type=F32)


def dot_nt(left, right):
    return lax.dot_general(left, right, (((1,), (1,)), ((), ())), preferred_element_type=F32)


def dot_tn(left, right):
    return lax.dot_general(left, right, (((0,), (0,)), ((), ())), preferred_element_type=F32)


def rms_scale(values, gain):
    return values * lax.rsqrt(jnp.mean(values * values, axis=-1, keepdims=True) + EPSILON) * gain


def softmax_rows(scores):
    row_top = jnp.max(scores, axis=-1, keepdims=True)
    expos = jnp.exp(scores - row_top)
    return expos / jnp.sum(expos, axis=-1, keepdims=True)


def gated_gelu(gate_part, up_part):
    return jax.nn.gelu(gate_part, approximate=True) * up_part


def shift_to(value, axis, steps):
    count = lax.axis_size(axis)
    return lax.ppermute(value, axis, [(source, (source + steps) % count) for source in range(count)])


def bias_rows(window, half, queries):
    width = queries + ROWS
    start = ROWS * (1 - half)
    part = jnp.broadcast_to(window[:, start : start + width], (ROWS, width))
    return pltpu.roll(part, width - ROWS, axis=1, stride=1, stride_axis=0)[:, :queries]


def attention_forward_kernel(q_ref, k0, k1, k2, k3, v0, v1, v2, v3, w_ref, o_ref, x_ref, l_ref, s_ref, p_ref):
    queries = q_ref[...]
    count = queries.shape[0]
    lanes = lax.broadcasted_iota(jnp.int32, queries.shape, 1)
    ks, vs = (k0, k1, k2, k3), (v0, v1, v2, v3)
    outs = []
    for head in range(2):
        own = (lanes < HEAD_DIM) if head == 0 else (lanes >= HEAD_DIM)
        q_head = jnp.where(own, queries, jnp.zeros_like(queries)) * jnp.asarray(1.0 / ROOT_SIZE, BF16)
        top = None
        for chunk in range(8):
            block, half = divmod(chunk, 2)
            rows = slice(half * ROWS, (half + 1) * ROWS)
            score = dot_nt(ks[block][rows, :], q_head)
            score = score + bias_rows(w_ref[head, block : block + 1, :], half, count)
            s_ref[chunk * ROWS : (chunk + 1) * ROWS, :] = score
            chunk_top = jnp.max(score, axis=0, keepdims=True)
            top = chunk_top if top is None else jnp.maximum(top, chunk_top)
        total = None
        for chunk in range(8):
            rows = slice(chunk * ROWS, (chunk + 1) * ROWS)
            expo = jnp.exp(s_ref[rows, :] - top)
            p_ref[rows, :] = expo.astype(BF16)
            part = jnp.sum(expo, axis=0, keepdims=True)
            total = part if total is None else total + part
        mixed = None
        for block in range(4):
            part = dot_tn(vs[block][...], p_ref[block * count : (block + 1) * count, :])
            mixed = part if mixed is None else mixed + part
        outs.append(mixed[head * HEAD_DIM : (head + 1) * HEAD_DIM, :] / total)
        l_ref[0, head : head + 1, :] = top + jnp.log(total)
    mixed_rows = jnp.concatenate(outs, axis=0).T
    o_ref[...] = mixed_rows.astype(BF16)
    x_ref[...] = mixed_rows


def attention_forward(queries, pairs_kv, windows):
    rows, width = queries.shape
    pairs = HEADS // 2
    pair = 2 * HEAD_DIM
    chunk_spec = pl.BlockSpec((rows, pair), lambda g: (0, g))
    value_spec = pl.BlockSpec((rows, pair), lambda g: (0, g + HEADS // 2))
    return pl.pallas_call(
        attention_forward_kernel,
        grid=(pairs,),
        in_specs=[chunk_spec] * 5
        + [value_spec] * 4
        + [pl.BlockSpec((2,) + windows.shape[1:], lambda g: (g, 0, 0))],
        out_specs=[chunk_spec, chunk_spec, pl.BlockSpec((1, 2, rows), lambda g: (g, 0, 0))],
        out_shape=[
            jax.ShapeDtypeStruct((rows, width), BF16),
            jax.ShapeDtypeStruct((rows, width), F32),
            jax.ShapeDtypeStruct((pairs, 2, rows), F32),
        ],
        scratch_shapes=[pltpu.VMEM((4 * rows, rows), F32), pltpu.VMEM((4 * rows, rows), BF16)],
        cost_estimate=pl.CostEstimate(
            flops=16 * rows * rows * width, bytes_accessed=20 * rows * width, transcendentals=4 * rows * rows * HEADS
        ),
        name="attention_forward",
    )(queries, *pairs_kv, *pairs_kv, windows)


def attention_backward_kernel(
    q_ref, g_ref, o_ref, l_ref, k0, k1, v0, v1, w_ref, *rest, given
):
    given_ref, rest = (rest[0], rest[1:]) if given else (None, rest)
    dq_ref, dkv0, dkv1, dw_ref, ds_ref, pb_ref, w8_ref = rest
    queries = q_ref[...]
    grads = g_ref[...]
    count = queries.shape[0]
    lanes = lax.broadcasted_iota(jnp.int32, queries.shape, 1)
    ks, vs, dkvs = (k0, k1), (v0, v1), (dkv0, dkv1)
    products = (grads.astype(F32) * o_ref[...]).T
    key_sums, value_sums, query_parts = [None] * 2, [None] * 2, []
    for head in range(2):
        own = (lanes < HEAD_DIM) if head == 0 else (lanes >= HEAD_DIM)
        place_head = slice(head * HEAD_DIM, (head + 1) * HEAD_DIM)
        q_head = jnp.where(own, queries, jnp.zeros_like(queries)) * jnp.asarray(1.0 / ROOT_SIZE, BF16)
        g_head = jnp.where(own, grads, jnp.zeros_like(grads))
        level = l_ref[0, head : head + 1, :]
        row_dot = jnp.sum(products[place_head, :], axis=0, keepdims=True)
        for chunk in range(4):
            block, half = divmod(chunk, 2)
            rows = slice(half * ROWS, (half + 1) * ROWS)
            place = slice(chunk * ROWS, (chunk + 1) * ROWS)
            score = dot_nt(ks[block][rows, :], q_head)
            score = score + bias_rows(w_ref[head, block : block + 1, :], half, count)
            attention = jnp.exp(score - level)
            pb_ref[place, :] = attention.astype(BF16)
            grad_attention = dot_nt(vs[block][rows, :], g_head)
            grad_score = (attention * (grad_attention - row_dot)).astype(BF16)
            ds_ref[place, :] = grad_score
            sheared = jnp.concatenate([grad_score.astype(F32), jnp.zeros((ROWS, ROWS), F32)], axis=1)
            live = ROWS
            while live > 8:
                live = live // 2
                sheared = pltpu.roll(sheared[:live, :], live, axis=1) + sheared[live:, :]
            start = ROWS * (1 - half)
            if half == 0:
                w8_ref[block, :, 0:ROWS] = jnp.zeros((8, ROWS), F32)
                w8_ref[block, :, start : start + count + ROWS] = sheared
            else:
                w8_ref[block, :, start : start + count + ROWS] += sheared
        query_part = None
        for block in range(2):
            place = slice(block * count, (block + 1) * count)
            part = dot_tn(ks[block][...], ds_ref[place, :])
            query_part = part if query_part is None else query_part + part
            key_part = matmul(ds_ref[place, :], q_head)
            value_part = matmul(pb_ref[place, :], g_head)
            if head == 0:
                key_sums[block], value_sums[block] = key_part, value_part
            else:
                dkvs[block][0] = (key_sums[block] + key_part).astype(dkvs[block].dtype)
                dkvs[block][1] = (value_sums[block] + value_part).astype(dkvs[block].dtype)
        query_parts.append(query_part[place_head, :])
        for block in range(2):
            folded = pltpu.roll(w8_ref[block], 1, axis=1)
            rows8 = lax.broadcasted_iota(jnp.int32, folded.shape, 0)
            for bit in (1, 2, 4):
                folded = jnp.where(jnp.bitwise_and(rows8, bit) == 0, pltpu.roll(folded, bit, axis=1), folded)
            dw_ref[head, block : block + 1, :] = jnp.sum(folded, axis=0, keepdims=True)
    grad_queries = jnp.concatenate(query_parts, axis=0).T * (1.0 / ROOT_SIZE)
    if given:
        grad_queries = grad_queries + given_ref[...]
    dq_ref[...] = grad_queries.astype(dq_ref.dtype)


def attention_backward(queries, grads, attended, levels, pairs_kv, windows, given=None):
    rows, width = queries.shape
    pairs = HEADS // 2
    pair = 2 * HEAD_DIM
    chunk_spec = pl.BlockSpec((rows, pair), lambda g: (0, g))
    value_spec = pl.BlockSpec((rows, pair), lambda g: (0, g + HEADS // 2))
    window_spec = pl.BlockSpec((2,) + windows.shape[1:], lambda g: (g, 0, 0))
    span = windows.shape[-1]
    extra = [] if given is None else [given]
    return pl.pallas_call(
        functools.partial(attention_backward_kernel, given=given is not None),
        grid=(pairs,),
        in_specs=[chunk_spec] * 3
        + [pl.BlockSpec((1, 2, rows), lambda g: (g, 0, 0))]
        + [chunk_spec] * 2
        + [value_spec] * 2
        + [window_spec]
        + [chunk_spec] * len(extra),
        out_specs=[chunk_spec]
        + [pl.BlockSpec((2, rows, pair), lambda g: (0, 0, g))] * 2
        + [pl.BlockSpec((2, 2, span), lambda g: (g, 0, 0))],
        out_shape=[
            jax.ShapeDtypeStruct((rows, width), F32 if given is None else BF16),
            jax.ShapeDtypeStruct((2, rows, width), F32),
            jax.ShapeDtypeStruct((2, rows, width), BF16),
            jax.ShapeDtypeStruct((HEADS, 2, span), F32),
        ],
        scratch_shapes=[
            pltpu.VMEM((2 * rows, rows), BF16),
            pltpu.VMEM((2 * rows, rows), BF16),
            pltpu.VMEM((2, 8, span), F32),
        ],
        cost_estimate=pl.CostEstimate(
            flops=20 * rows * rows * width, bytes_accessed=36 * rows * width, transcendentals=2 * rows * rows * HEADS
        ),
        name="attention_backward",
    )(queries, grads, attended, levels, *pairs_kv, *pairs_kv, windows, *extra)


def section_swap(value):
    return lax.ppermute(value, SECTION, [(0, 1), (1, 0)])


def inner_swap(value):
    return shift_to(value, INNER, 1)


def outer_swap(value):
    return shift_to(value, OUTER, 1)


def rms_pull(values, gain, grad):
    scale = lax.rsqrt(jnp.mean(values * values, axis=-1, keepdims=True) + EPSILON)
    weighted = grad * gain
    lean = jnp.mean(weighted * values, axis=-1, keepdims=True)
    grad_values = scale * weighted - values * (scale * scale * scale * lean)
    grad_gain = jnp.sum(grad * values * scale, axis=0)
    return grad_values, grad_gain


def send_slots(rows, direction):
    count = lax.axis_size(EXPERT)
    parts = [rows[0]] + [shift_to(rows[k], EXPERT, direction * k) for k in range(1, count)]
    return jnp.concatenate(parts, axis=0)


def route_tables(route, capacity):
    tokens = route.shape[0]
    count = lax.axis_size(EXPERT)
    ahead = jnp.remainder(route - lax.axis_index(EXPERT) + count, count)
    onehot = (ahead[:, :, None] == jnp.arange(count, dtype=jnp.int32)).astype(F32)
    per_row = jnp.sum(onehot, axis=1)
    earlier = (jnp.arange(tokens)[:, None] > jnp.arange(tokens)[None, :]).astype(BF16)
    before = matmul(earlier, per_row.astype(BF16))
    slot_place = jnp.sum(before[:, None, :] * onehot, axis=2).astype(jnp.int32)
    target = ahead * capacity + slot_place
    slots = jnp.arange(count * capacity, dtype=jnp.int32)
    spots = (target[:, 0:1] == slots) | (target[:, 1:2] == slots)
    owner = jnp.remainder(slots // capacity + lax.axis_index(EXPERT), count)
    members = (owner[:, None] == jnp.arange(count, dtype=jnp.int32)).astype(F32)
    return spots, members


def forward(section_in, tables, weights, windows, started):
    spots, members = tables
    slot_table = spots.astype(BF16)
    slot_count = slot_table.shape[1]
    expert_count = lax.axis_size(EXPERT)
    inputs = section_in.astype(F32)
    width = inputs.shape[1]
    if started is None:
        normed = rms_scale(inputs, weights["gain_first"]).astype(BF16)
        pair_own = matmul(normed, weights["pair"]).astype(BF16)
        pair_outer = outer_swap(pair_own)
    else:
        normed, pair_own, pair_outer = started
    pair_inner = inner_swap(pair_own)
    queries = matmul(normed, weights["query"]).astype(BF16)
    pair_both = inner_swap(pair_outer)
    pairs_kv = (pair_own, pair_inner, pair_outer, pair_both)
    attended, attended_full, levels = attention_forward(queries, pairs_kv, windows)
    middle = inputs + matmul(attended, weights["output"])
    mixed_in = rms_scale(middle, weights["gain_second"]).astype(BF16)
    packed = dot_tn(slot_table, mixed_in).astype(BF16)
    arrived = send_slots(packed.reshape(expert_count, -1, width), 1)
    gates_all = softmax_rows(matmul(mixed_in, weights["router"]))
    spread = lax.dot_general(
        gates_all, members, (((1,), (1,)), ((), ())), precision=lax.Precision.HIGHEST, preferred_element_type=F32
    )
    combine = jnp.where(spots, spread, 0.0)
    combine_high = combine.astype(BF16)
    combine_low = (combine - combine_high.astype(F32)).astype(BF16)
    gate_part = matmul(arrived, weights["gate"])
    up_part = matmul(arrived, weights["up"])
    hidden = gated_gelu(gate_part, up_part).astype(BF16)
    produced = dot_nt(hidden, weights["down"]).astype(BF16)
    returned = send_slots(produced.reshape(expert_count, -1, width), -1)
    mixed_out = matmul(combine_high, returned) + matmul(combine_low, returned)
    result = (middle + mixed_out).astype(BF16)
    stored = (
        inputs, normed, queries, pairs_kv, attended, attended_full, levels, middle, mixed_in, gates_all,
        arrived, gate_part, up_part, hidden, returned, combine_high, combine_low,
    )
    return result, stored


def backward(grad_rows, stored, tables, weights, windows, bucket_rows, source, waited):
    spots, members = tables
    slot_table = spots.astype(BF16)
    (
        inputs, normed, queries, pairs_kv, attended, attended_full, levels, middle, mixed_in, gates_all,
        arrived, gate_part, up_part, hidden, returned, combine_high, combine_low,
    ) = stored
    expert_count = lax.axis_size(EXPERT)
    width = inputs.shape[1]
    grad_out = grad_rows.astype(F32)
    grad_slots = (dot_tn(combine_high, grad_rows) + dot_tn(combine_low, grad_rows)).astype(BF16)
    if source == 0:
        grad_slots, arrived = lax.optimization_barrier((grad_slots, arrived))
    received = send_slots(grad_slots.reshape(expert_count, -1, width), 1)
    received, waited[0] = lax.optimization_barrier((received, waited[0]))
    def for_inner(left, right):
        return dot_tn(inner_columns(left, 1), right).astype(BF16)

    def from_inner(term):
        return inner_swap(term).reshape(2, -1, term.shape[1])

    def for_outer(left, right, taken):
        return plus(dot_tn(replica_columns(left, 1), right), take(taken, 1 - lax.axis_index(OUTER), 0))

    down_given, received = lax.optimization_barrier((for_inner(received, hidden), received))
    down_inner = from_inner(down_given)
    grad_hidden = matmul(received, weights["down"])
    unused_value, pull_gelu = jax.vjp(gated_gelu, gate_part, up_part)
    grad_gate, grad_up = pull_gelu(grad_hidden)
    grad_gate, grad_up, down_inner, returned = lax.optimization_barrier(
        (grad_gate.astype(BF16), grad_up.astype(BF16), down_inner, returned)
    )
    products = jnp.where(spots, dot_nt(grad_rows, returned), 0.0)
    grad_gates = jnp.dot(products, members, precision=lax.Precision.HIGHEST, preferred_element_type=F32)
    grad_logits = gates_all * (grad_gates - jnp.sum(gates_all * grad_gates, axis=-1, keepdims=True))
    grad_logits = grad_logits.astype(BF16)
    term_router = dot_tn(mixed_in, grad_logits)

    grad_gate, grad_up, down_given = lax.optimization_barrier(
        (grad_gate, grad_up, for_outer(received, hidden, down_inner))
    )
    down_outer = outer_swap(down_given)
    gate_given, up_given, grad_gate, grad_up = lax.optimization_barrier(
        (for_inner(arrived, grad_gate), for_inner(arrived, grad_up), grad_gate, grad_up)
    )
    gate_inner, up_inner = from_inner(gate_given), from_inner(up_given)
    grad_arrived = (dot_nt(grad_gate, weights["gate"]) + dot_nt(grad_up, weights["up"])).astype(BF16)
    grad_arrived, gate_inner, up_inner = lax.optimization_barrier((grad_arrived, gate_inner, up_inner))
    back_rows = send_slots(grad_arrived.reshape(expert_count, -1, width), -1)
    gate_given = for_outer(arrived, grad_gate, gate_inner)
    up_given = for_outer(arrived, grad_up, up_inner)
    back_rows, gate_given, up_given, down_outer, waited[1], waited[5] = lax.optimization_barrier(
        (back_rows, gate_given, up_given, down_outer, waited[1], waited[5])
    )
    gate_outer = outer_swap(gate_given)
    if source == 1:
        waited[5] = reduce_dense(waited[5])
    share_down = finish_expert(received, hidden, down_inner, down_outer)

    grad_mixed = matmul(slot_table, back_rows) + dot_nt(grad_logits, weights["router"])
    grad_middle, term_second = rms_pull(middle, weights["gain_second"], grad_mixed)
    grad_middle = grad_middle + grad_out
    grad_branch = grad_middle.astype(BF16)
    grad_attended = dot_nt(grad_branch, weights["output"]).astype(BF16)
    term_output = dot_tn(attended, grad_branch).astype(BF16)
    grad_attended, share_down, waited[2] = lax.optimization_barrier((grad_attended, share_down, waited[2]))
    hop_down = lax.ppermute(share_down, SECTION, [(source, 1 - source)])
    grad_part, outer, both, windows_far = attention_backward(
        queries, grad_attended, attended_full, levels, pairs_kv[2:], windows[:, 2:]
    )
    far_taken = inner_swap(both)
    grad_part, far_taken, gate_outer, waited[3] = lax.optimization_barrier(
        (grad_part, far_taken, gate_outer, waited[3])
    )
    passed = plus(outer, far_taken)
    passed, grad_part = lax.optimization_barrier((passed, grad_part))
    outer_sum = outer_swap(passed)
    grad_queries, own, inner, windows_near = attention_backward(
        queries, grad_attended, attended_full, levels, pairs_kv[:2], windows[:, :2], grad_part
    )
    share_gate = finish_expert(arrived, grad_gate, gate_inner, gate_outer)
    even = lax.axis_index(INNER) == 0
    lefts, rights = (attended, normed), (grad_branch, grad_queries)
    given = dot_tn(jnp.where(even, *lefts[::-1]), jnp.where(even, *rights[::-1])).astype(BF16)
    grad_queries, own, inner, outer_sum, share_gate, given, waited[4] = lax.optimization_barrier(
        (grad_queries, own, inner, outer_sum, share_gate, given, waited[4])
    )
    first_taken = inner_swap(given)
    up_given, own = lax.optimization_barrier((up_given, own))
    up_outer = outer_swap(up_given)
    grad_windows = jnp.concatenate([windows_near, windows_far], axis=1)
    near_sum = own + inner_swap(inner).astype(F32)
    grad_windows = grad_windows.reshape(HEADS, -1)
    term_position = lax.dot_general(
        grad_windows, bucket_rows.astype(F32), (((1,), (1,)), ((), ())),
        precision=lax.Precision.HIGHEST, preferred_element_type=F32,
    )
    grad_normed = dot_nt(grad_queries, weights["query"])
    small_early = (term_router, term_second, term_position)
    grad_pair = (near_sum + outer_sum.astype(F32)).astype(BF16)
    index = lax.axis_index(INNER)
    given = dot_tn(normed, take(grad_pair, 1 - index, 0)).astype(BF16)
    grad_pair, grad_normed, first_taken, given, small_early, waited[5] = lax.optimization_barrier(
        (grad_pair, grad_normed, first_taken, given, small_early, waited[5])
    )
    second_taken = inner_swap(given)
    count = lax.axis_size(EXPERT)
    first_sum = plus(dot_tn(jnp.where(even, *lefts), jnp.where(even, *rights)), first_taken)
    first_sum = first_sum.reshape(2 * count, -1, width)
    grad_normed = grad_normed + dot_nt(grad_pair[0], weights["key"]) + dot_nt(grad_pair[1], weights["value"])
    grad_in, term_first = rms_pull(inputs, weights["gain_first"], grad_normed)
    grad_in = grad_in + grad_middle
    grad_rows = grad_in.astype(BF16)
    small = pack_small(small_early[0], term_first, small_early[1], small_early[2], count).astype(BF16)
    small = small.reshape(2 * count, -1, width)
    small = jnp.pad(small, ((0, 0), (0, 16 - small.shape[1]), (0, 0)))
    second_sum = plus(dot_tn(normed, take(grad_pair, index, 0)), second_taken)
    second_sum = jnp.concatenate([second_sum.reshape(2 * count, -1, width), small], axis=1)
    if source == 0:
        dense = jnp.concatenate([first_sum, second_sum], axis=1)
        grad_rows, dense = lax.optimization_barrier((grad_rows, dense))
    else:
        dense = (reduce_dense(first_sum), fold_dense(second_sum))
    share_up = finish_expert(arrived, grad_up, up_inner, up_outer)
    return grad_in, grad_rows, dense, (share_gate, share_up, share_down), hop_down, waited


def reduce_dense(blocks):
    return lax.psum_scatter(blocks, (EXPERT, OUTER), scatter_dimension=0, tiled=False)


def fold_dense(blocks):
    count = lax.axis_size(EXPERT)
    expert_index, outer_index = lax.axis_index(EXPERT), lax.axis_index(OUTER)
    blocks = blocks.reshape(count, 2, -1, blocks.shape[-1])
    part = plus(take(blocks, outer_index, 1), outer_swap(take(blocks, 1 - outer_index, 1)))
    total = take(part, expert_index, 0).astype(F32)
    for ahead in range(1, count):
        given = take(part, jnp.remainder(expert_index + ahead, count), 0)
        total = total + shift_to(given, EXPERT, ahead).astype(F32)
    total = total.astype(BF16)
    total = plus(total, lax.ppermute(total, SECTION, [(1, 0)]))
    partner = outer_swap(total)
    lower, even = outer_index == 0, lax.axis_index(INNER) == 0
    own = jnp.where(lower, jnp.stack([total, partner]), jnp.stack([partner, total]))
    other = inner_swap(own)
    return jnp.where(even, jnp.stack([own, other]), jnp.stack([other, own]))


def finish_expert(left, right, taken, last):
    return plus(dot_tn(replica_columns(left, 0), right) + take(taken, lax.axis_index(OUTER), 0).astype(F32), last)


def take(blocks, index, axis):
    return lax.dynamic_index_in_dim(blocks, index, axis, keepdims=False)


def plus(left, right):
    return (left.astype(F32) + right.astype(F32)).astype(BF16)


def pick_columns(values, index, size, count):
    parts = [
        lax.dynamic_slice_in_dim(values, start + index * size, size, 1)
        for start in range(0, values.shape[1], size * count)
    ]
    return jnp.concatenate(parts, axis=1)


def inner_columns(values, other):
    return pick_columns(values, jnp.bitwise_xor(lax.axis_index(INNER), other), values.shape[1] // 4, 2)


def replica_columns(values, other):
    width = values.shape[1] // 4
    place = 2 * jnp.bitwise_xor(lax.axis_index(OUTER), other) + lax.axis_index(INNER)
    return lax.dynamic_slice_in_dim(values, place * width, width, 1)


def pack_small(router, first, second, position, count):
    parts = [router.reshape(count, -1), first.reshape(count, -1), second.reshape(count, -1), position.reshape(count, -1)]
    flat = jnp.concatenate(parts, axis=1)
    return jnp.pad(flat, ((0, 0), (0, -flat.shape[1] % 1024)))


def unpack_small(flat, rows, experts, heads, buckets):
    sizes = [rows * experts, rows, rows, heads * buckets]
    starts = [sum(sizes[:k]) for k in range(5)]
    pieces = [flat[:, starts[k] : starts[k + 1]] for k in range(4)]
    return pieces[0].reshape(-1, experts), pieces[1].reshape(-1), pieces[2].reshape(-1), pieces[3].reshape(-1, buckets)


def shards(
    inputs,
    cotangent,
    routes,
    bucket_table,
    query_weight,
    key_weight,
    value_weight,
    output_weight,
    router_weight,
    attention_gain,
    mixture_gain,
    position_bias,
    expert_gate,
    expert_up,
    expert_down,
):
    micro_count = inputs.shape[0]
    tok_rows = inputs.shape[2]
    model_width = inputs.shape[3]
    expert_count = lax.axis_size(EXPERT)
    replica_count = lax.axis_size(OUTER) * lax.axis_size(INNER)
    assert micro_count == lax.axis_size(SECTION) == 2 and replica_count == 4
    capacity = max(2, 9 * tok_rows // (4 * expert_count))
    length = tok_rows * replica_count
    buckets = position_bias.shape[2]
    section_index = lax.axis_index(SECTION)
    replica_index = 2 * lax.axis_index(OUTER) + lax.axis_index(INNER)
    first_section = section_index == 0

    own_rows = lax.dynamic_index_in_dim(inputs[:, 0], section_index, 0, keepdims=False)
    own_cotangent = lax.dynamic_index_in_dim(cotangent[:, 0], section_index, 0, keepdims=False)
    layer_routes = routes[0, :, 0]
    route_kept = lax.dynamic_index_in_dim(layer_routes, section_index, 0, keepdims=False)
    route_given = lax.dynamic_index_in_dim(layer_routes, 1 - section_index, 0, keepdims=False)
    route_taken = section_swap(route_given)
    layer_route = (
        jnp.where(first_section, route_kept, route_taken),
        jnp.where(first_section, route_taken, route_kept),
    )

    dense_rows = query_weight.shape[1]
    inner_index = lax.axis_index(INNER)
    expert_index = lax.axis_index(EXPERT)
    half_rows = dense_rows // 2

    def half_piece(*own_parts):
        return jnp.concatenate(
            [lax.dynamic_slice_in_dim(part, inner_index * half_rows, half_rows, 0) for part in own_parts], axis=1
        )

    def from_first(own):
        return jnp.where(first_section, own, lax.ppermute(own, SECTION, [(0, 1)]))

    def half_of(part, index):
        return lax.dynamic_slice_in_dim(part, index * (part.shape[0] // 2), part.shape[0] // 2, 0)

    def ring_gather(piece, joined=(), at=None):
        whole = jnp.zeros((model_width, piece.shape[1]), BF16)
        for step in range(expert_count):
            start = jnp.remainder(expert_index - step + expert_count, expert_count) * dense_rows
            whole = lax.dynamic_update_slice(whole, piece, (start + inner_index * half_rows, 0))
            whole = lax.dynamic_update_slice(whole, inner_swap(piece), (start + (1 - inner_index) * half_rows, 0))
            if step + 1 < expert_count:
                piece = shift_to(piece, EXPERT, 1)
            if step == at:
                piece, joined = lax.optimization_barrier((piece, joined))
        return whole, joined

    def half_of(part, index):
        return lax.dynamic_slice_in_dim(part, index * (part.shape[0] // 2), part.shape[0] // 2, 0)

    small_own = pack_small(router_weight[0], attention_gain[0], mixture_gain[0], position_bias[0], 1)[0]
    small_taken = section_swap(small_own)
    pair_piece = from_first(half_piece(key_weight[0], value_weight[0]))
    small_piece = jnp.where(
        first_section, jnp.stack([small_own, small_taken]), jnp.stack([small_taken, small_own])
    ).reshape(2, 1, -1)
    small_all = jnp.zeros((2, expert_count, small_piece.shape[2]), BF16)
    for step in range(expert_count):
        source = jnp.remainder(expert_index - step + expert_count, expert_count)
        small_all = lax.dynamic_update_slice(small_all, small_piece, (0, source, 0))
        if step + 1 < expert_count:
            small_piece = shift_to(small_piece, EXPERT, 1)

    second_own, pair_piece = lax.optimization_barrier(
        (half_piece(query_weight[0], output_weight[0]), pair_piece)
    )
    wide_own = (expert_gate[0, 0], expert_up[0, 0], expert_down[0, 0].T)
    wide_kept = jnp.concatenate([half_of(part, section_index) for part in wide_own], axis=1)
    wide_sent = jnp.concatenate([half_of(part, 1 - section_index) for part in wide_own], axis=1)
    wide_sent, pair_piece = lax.optimization_barrier((wide_sent, pair_piece))
    wide_taken = section_swap(wide_sent)
    second_half = from_first(second_own)
    first_pair, wide_taken = ring_gather(pair_piece, wide_taken, expert_count - 2 if expert_count > 1 else 0)
    first_pair, small_all, second_half = lax.optimization_barrier((first_pair, small_all, second_half))
    small_parts = [
        unpack_small(small_all[layer], dense_rows, expert_count, position_bias.shape[1], position_bias.shape[2])
        for layer in range(2)
    ]
    normed = rms_scale(own_rows.astype(F32), small_parts[0][1].astype(F32)).astype(BF16)
    first_own = matmul(normed, first_pair).astype(BF16)
    second_half, first_own = lax.optimization_barrier((second_half, first_own))
    first_outer = outer_swap(first_own)
    second_whole, unused = ring_gather(second_half)
    second_whole, first_outer = lax.optimization_barrier((second_whole, first_outer))
    first_query, first_output = second_whole[:, :model_width], second_whole[:, model_width:]

    eighth = dense_rows // 8

    def by_layer(kept_part, taken_part):
        return jnp.where(first_section, kept_part, taken_part), jnp.where(first_section, taken_part, kept_part)

    dense_axes = (EXPERT, SECTION) + REPLICA

    def eighths(*parts):
        kept_part = jnp.concatenate(
            [lax.dynamic_slice_in_dim(part, (4 * section_index + replica_index) * eighth, eighth, 0) for part in parts],
            axis=1,
        )
        sent_part = jnp.concatenate(
            [lax.dynamic_slice_in_dim(part, (4 * (1 - section_index) + replica_index) * eighth, eighth, 0) for part in parts],
            axis=1,
        )
        return kept_part, sent_part

    hidden_width = expert_gate.shape[3]
    rest_kept, rest_sent = eighths(key_weight[0], value_weight[0], query_weight[0], output_weight[0])
    rest_sent, first_own = lax.optimization_barrier((rest_sent, first_own))
    second_piece = by_layer(rest_kept, section_swap(rest_sent))[1]
    second_piece, first_query, first_own = lax.optimization_barrier((second_piece, first_query, first_own))
    heads_own = position_bias.shape[1]
    wide_pieces = by_layer(wide_kept, wide_taken)
    wide_all = []
    wide_all.append(lax.all_gather(wide_pieces[0], REPLICA + (SECTION,), axis=0, tiled=True))
    second_all = lax.all_gather(second_piece, dense_axes, axis=0, tiled=True)
    wide_all.append(lax.all_gather(wide_pieces[1], REPLICA + (SECTION,), axis=0, tiled=True))
    dense_all = (
        (first_pair, first_query, first_output),
        tuple(second_all[:, a * model_width : z * model_width] for a, z in ((0, 2), (2, 3), (3, 4))),
    )

    reversed_table = jnp.concatenate([jnp.full((1,), -1, jnp.int32), bucket_table[::-1]])
    bucket_onehot = (jnp.arange(buckets, dtype=jnp.int32)[:, None] == reversed_table[None, :]).astype(BF16)
    bucket_rows = jnp.concatenate(
        [
            lax.dynamic_slice(
                bucket_onehot,
                (0, (3 + replica_index - jnp.bitwise_xor(replica_index, ahead)) * tok_rows),
                (buckets, 2 * tok_rows),
            )
            for ahead in range(4)
        ],
        axis=1,
    )

    layers = []
    for layer in range(2):
        router, first, second, position = small_parts[layer]
        weights = dict(
            pair=dense_all[layer][0],
            key=dense_all[layer][0][:, :model_width],
            value=dense_all[layer][0][:, model_width:],
            query=dense_all[layer][1],
            output=dense_all[layer][2],
            router=router,
            gain_first=first.astype(F32),
            gain_second=second.astype(F32),
            gate=wide_all[layer][:, :hidden_width],
            up=wide_all[layer][:, hidden_width : 2 * hidden_width],
            down=wide_all[layer][:, 2 * hidden_width :],
        )
        windows = matmul(position, bucket_rows).reshape(HEADS, 4, 2 * tok_rows)
        layers.append((weights, windows, route_tables(layer_route[layer], capacity)))

    rows, outputs, kept = own_rows, [], []
    for weights, windows, tables in layers:
        rows, stored = forward(rows, tables, weights, windows, (normed, first_own, first_outer) if not kept else None)
        outputs.append(rows)
        kept.append(stored)

    weights, windows, tables = layers[1]
    grad_in_one, grads, dense_one, shares_one, hop_down_one, waited = backward(
        own_cotangent, kept[1], tables, weights, windows, bucket_rows, 0, [()] * 6
    )
    hop_gate_one, hop_up_one = (lax.ppermute(share, SECTION, [(0, 1)]) for share in shares_one[:2])
    grad_from_one = lax.ppermute(grads, SECTION, [(0, 1)])

    weights, windows, tables = layers[0]
    output_taken = section_swap(jnp.where(first_section, outputs[1], outputs[0]))
    waited = [(hop_down_one, output_taken), shares_one, (), hop_gate_one, (), dense_one]
    grad_in_zero, grads, dense_zero, shares_zero, hop_down_zero, waited = backward(
        grads, kept[0], tables, weights, windows, bucket_rows, 1, waited
    )
    (hop_down_one, output_taken), shares_one, unused, hop_gate_one, unused, dense_one = waited
    hops_one = (hop_gate_one, hop_up_one, hop_down_one)
    hop_gate_zero, hop_up_zero = (lax.ppermute(share, SECTION, [(1, 0)]) for share in shares_zero[:2])
    early_zero, late_zero = dense_zero
    half_count = dense_rows // 2
    early_taken = lax.ppermute(early_zero, SECTION, [(1, 0)])
    one_taken = lax.ppermute(dense_one, SECTION, [(0, 1)])
    early_own = jnp.where(
        first_section, plus(early_zero, early_taken), plus(dense_one[:half_count], one_taken[:half_count])
    )
    dense_own = jnp.concatenate([early_own, plus(dense_one[half_count:], one_taken[half_count:])], axis=0)
    hops_zero = (hop_gate_zero, hop_up_zero, hop_down_zero)
    final_gate, final_up, final_down = (
        jnp.where(first_section, zero, one).astype(F32) + jnp.where(first_section, zero_hop, one_hop).astype(F32)
        for zero, zero_hop, one, one_hop in zip(shares_zero, hops_zero, shares_one, hops_one)
    )
    final_dense = lax.all_gather(dense_own, REPLICA, axis=0, tiled=False).reshape(2, 2, -1, model_width)
    late_own = jnp.where(first_section, late_zero, final_dense[:, :, half_count:].transpose(1, 0, 2, 3))
    final_output, final_query = (
        final_dense[:, inner, :half_count].reshape(dense_rows, model_width).astype(F32) for inner in range(2)
    )
    final_key, final_value = (
        late_own[inner, :, :half_count].reshape(dense_rows, model_width).astype(F32) for inner in range(2)
    )
    small_rows = late_own[:, :, half_count:].astype(F32)
    small_rows = (small_rows[0] + small_rows[1]).reshape(2, -1)
    small_length = small_own.shape[0]
    small_rows = small_rows[:, : small_length // 2].reshape(1, -1)
    final_router, final_first, final_second, final_position = unpack_small(
        small_rows, dense_rows, expert_count, heads_own, buckets
    )

    def both_micros(kept_one, taken_one):
        return jnp.where(
            first_section, jnp.stack([kept_one, taken_one]), jnp.stack([taken_one, kept_one])
        )[None, :, None]

    section_output = both_micros(jnp.where(first_section, outputs[0], outputs[1]), output_taken)
    grad_from_zero = lax.ppermute(grads, SECTION, [(1, 0)])
    grad_taken = jnp.where(first_section, grad_from_zero, grad_from_one).astype(F32)
    grad_kept = jnp.where(first_section, grad_in_zero, grad_in_one)
    input_gradient = both_micros(grad_kept, grad_taken)
    return (
        section_output,
        input_gradient,
        final_query[None],
        final_key[None],
        final_value[None],
        final_output[None],
        final_router[None],
        final_first[None],
        final_second[None],
        final_position[None],
        final_gate[None, None],
        final_up[None, None],
        final_down.T[None, None],
    )


def solution(mesh):
    sections, experts, replicas = (mesh.shape[name] for name in ("section", "expert", "replica"))
    fine = Mesh(
        mesh.devices.reshape(sections, experts, replicas // 2, 2), (SECTION, EXPERT, OUTER, INNER)
    )
    rep = REPLICA
    in_specs = (
        P(None, "expert", rep, None),
        P(None, "expert", rep, None),
        P("section", None, "expert", rep, None),
        P(),
        P("section", "expert", None),
        P("section", "expert", None),
        P("section", "expert", None),
        P("section", "expert", None),
        P("section", "expert", None),
        P("section", "expert"),
        P("section", "expert"),
        P("section", "expert", None),
        P("section", "expert", rep, None),
        P("section", "expert", rep, None),
        P("section", "expert", None, rep),
    )
    out_specs = (
        P("section", None, "expert", rep, None),
        P("section", None, "expert", rep, None),
        P("section", "expert", None),
        P("section", "expert", None),
        P("section", "expert", None),
        P("section", "expert", None),
        P("section", "expert", None),
        P("section", "expert"),
        P("section", "expert"),
        P("section", "expert", None),
        P("section", "expert", rep, None),
        P("section", "expert", rep, None),
        P("section", "expert", None, rep),
    )
    return jax.shard_map(shards, mesh=fine, in_specs=in_specs, out_specs=out_specs, check_vma=False)
```

```python
import functools
import math

import jax
import jax.numpy as jnp
from jax import lax
from jax.experimental import pallas as pl
from jax.experimental.pallas import tpu as pltpu
from jax.sharding import Mesh
from jax.sharding import PartitionSpec as P

HEADS = 16
HEAD_DIM = 64
EPSILON = 1e-06
ROOT_SIZE = math.sqrt(HEAD_DIM)

SECTION = "section"
EXPERT = "expert"
OUTER = "outer"
INNER = "inner"
REPLICA = (OUTER, INNER)

BF16 = jnp.bfloat16
F32 = jnp.float32
ROWS = 128


def matmul(left, right):
    return jnp.dot(left, right, preferred_element_type=F32)


def dot_nt(left, right):
    return lax.dot_general(left, right, (((1,), (1,)), ((), ())), preferred_element_type=F32)


def dot_tn(left, right):
    return lax.dot_general(left, right, (((0,), (0,)), ((), ())), preferred_element_type=F32)


def rms_scale(values, gain):
    return values * lax.rsqrt(jnp.mean(values * values, axis=-1, keepdims=True) + EPSILON) * gain


def softmax_rows(scores):
    row_top = jnp.max(scores, axis=-1, keepdims=True)
    expos = jnp.exp(scores - row_top)
    return expos / jnp.sum(expos, axis=-1, keepdims=True)


def gated_gelu(gate_part, up_part):
    return jax.nn.gelu(gate_part, approximate=True) * up_part


def shift_to(value, axis, steps):
    count = lax.axis_size(axis)
    return lax.ppermute(value, axis, [(source, (source + steps) % count) for source in range(count)])


def bias_rows(window, half, queries):
    width = queries + ROWS
    start = ROWS * (1 - half)
    part = jnp.broadcast_to(window[:, start : start + width], (ROWS, width))
    return pltpu.roll(part, width - ROWS, axis=1, stride=1, stride_axis=0)[:, :queries]


def attention_forward_kernel(q_ref, k0, k1, k2, k3, v0, v1, v2, v3, w_ref, o_ref, x_ref, l_ref, s_ref, p_ref):
    queries = q_ref[...]
    count = queries.shape[0]
    lanes = lax.broadcasted_iota(jnp.int32, queries.shape, 1)
    ks, vs = (k0, k1, k2, k3), (v0, v1, v2, v3)
    outs = []
    for head in range(2):
        own = (lanes < HEAD_DIM) if head == 0 else (lanes >= HEAD_DIM)
        q_head = jnp.where(own, queries, jnp.zeros_like(queries)) * jnp.asarray(1.0 / ROOT_SIZE, BF16)
        top = None
        for chunk in range(8):
            block, half = divmod(chunk, 2)
            rows = slice(half * ROWS, (half + 1) * ROWS)
            score = dot_nt(ks[block][rows, :], q_head)
            score = score + bias_rows(w_ref[head, block : block + 1, :], half, count)
            s_ref[chunk * ROWS : (chunk + 1) * ROWS, :] = score
            chunk_top = jnp.max(score, axis=0, keepdims=True)
            top = chunk_top if top is None else jnp.maximum(top, chunk_top)
        total = None
        for chunk in range(8):
            rows = slice(chunk * ROWS, (chunk + 1) * ROWS)
            expo = jnp.exp(s_ref[rows, :] - top)
            p_ref[rows, :] = expo.astype(BF16)
            part = jnp.sum(expo, axis=0, keepdims=True)
            total = part if total is None else total + part
        mixed = None
        for block in range(4):
            part = dot_tn(vs[block][...], p_ref[block * count : (block + 1) * count, :])
            mixed = part if mixed is None else mixed + part
        outs.append(mixed[head * HEAD_DIM : (head + 1) * HEAD_DIM, :] / total)
        l_ref[0, head : head + 1, :] = top + jnp.log(total)
    mixed_rows = jnp.concatenate(outs, axis=0).T
    o_ref[...] = mixed_rows.astype(BF16)
    x_ref[...] = mixed_rows


def attention_forward(queries, pairs_kv, windows):
    rows, width = queries.shape
    pairs = HEADS // 2
    pair = 2 * HEAD_DIM
    chunk_spec = pl.BlockSpec((rows, pair), lambda g: (0, g))
    value_spec = pl.BlockSpec((rows, pair), lambda g: (0, g + HEADS // 2))
    return pl.pallas_call(
        attention_forward_kernel,
        grid=(pairs,),
        in_specs=[chunk_spec] * 5
        + [value_spec] * 4
        + [pl.BlockSpec((2,) + windows.shape[1:], lambda g: (g, 0, 0))],
        out_specs=[chunk_spec, chunk_spec, pl.BlockSpec((1, 2, rows), lambda g: (g, 0, 0))],
        out_shape=[
            jax.ShapeDtypeStruct((rows, width), BF16),
            jax.ShapeDtypeStruct((rows, width), F32),
            jax.ShapeDtypeStruct((pairs, 2, rows), F32),
        ],
        scratch_shapes=[pltpu.VMEM((4 * rows, rows), F32), pltpu.VMEM((4 * rows, rows), BF16)],
        cost_estimate=pl.CostEstimate(
            flops=16 * rows * rows * width, bytes_accessed=20 * rows * width, transcendentals=4 * rows * rows * HEADS
        ),
        name="attention_forward",
    )(queries, *pairs_kv, *pairs_kv, windows)


def attention_backward_kernel(
    q_ref, g_ref, o_ref, l_ref, k0, k1, v0, v1, w_ref, *rest, given
):
    given_ref, rest = (rest[0], rest[1:]) if given else (None, rest)
    dq_ref, dkv0, dkv1, dw_ref, ds_ref, pb_ref, w8_ref = rest
    queries = q_ref[...]
    grads = g_ref[...]
    count = queries.shape[0]
    lanes = lax.broadcasted_iota(jnp.int32, queries.shape, 1)
    ks, vs, dkvs = (k0, k1), (v0, v1), (dkv0, dkv1)
    products = (grads.astype(F32) * o_ref[...]).T
    key_sums, value_sums, query_parts = [None] * 2, [None] * 2, []
    for head in range(2):
        own = (lanes < HEAD_DIM) if head == 0 else (lanes >= HEAD_DIM)
        place_head = slice(head * HEAD_DIM, (head + 1) * HEAD_DIM)
        q_head = jnp.where(own, queries, jnp.zeros_like(queries)) * jnp.asarray(1.0 / ROOT_SIZE, BF16)
        g_head = jnp.where(own, grads, jnp.zeros_like(grads))
        level = l_ref[0, head : head + 1, :]
        row_dot = jnp.sum(products[place_head, :], axis=0, keepdims=True)
        for chunk in range(4):
            block, half = divmod(chunk, 2)
            rows = slice(half * ROWS, (half + 1) * ROWS)
            place = slice(chunk * ROWS, (chunk + 1) * ROWS)
            score = dot_nt(ks[block][rows, :], q_head)
            score = score + bias_rows(w_ref[head, block : block + 1, :], half, count)
            attention = jnp.exp(score - level)
            pb_ref[place, :] = attention.astype(BF16)
            grad_attention = dot_nt(vs[block][rows, :], g_head)
            grad_score = (attention * (grad_attention - row_dot)).astype(BF16)
            ds_ref[place, :] = grad_score
            sheared = jnp.concatenate([grad_score.astype(F32), jnp.zeros((ROWS, ROWS), F32)], axis=1)
            live = ROWS
            while live > 8:
                live = live // 2
                sheared = pltpu.roll(sheared[:live, :], live, axis=1) + sheared[live:, :]
            start = ROWS * (1 - half)
            if half == 0:
                w8_ref[block, :, 0:ROWS] = jnp.zeros((8, ROWS), F32)
                w8_ref[block, :, start : start + count + ROWS] = sheared
            else:
                w8_ref[block, :, start : start + count + ROWS] += sheared
        query_part = None
        for block in range(2):
            place = slice(block * count, (block + 1) * count)
            part = dot_tn(ks[block][...], ds_ref[place, :])
            query_part = part if query_part is None else query_part + part
            key_part = matmul(ds_ref[place, :], q_head)
            value_part = matmul(pb_ref[place, :], g_head)
            if head == 0:
                key_sums[block], value_sums[block] = key_part, value_part
            else:
                dkvs[block][0] = (key_sums[block] + key_part).astype(dkvs[block].dtype)
                dkvs[block][1] = (value_sums[block] + value_part).astype(dkvs[block].dtype)
        query_parts.append(query_part[place_head, :])
        for block in range(2):
            folded = pltpu.roll(w8_ref[block], 1, axis=1)
            rows8 = lax.broadcasted_iota(jnp.int32, folded.shape, 0)
            for bit in (1, 2, 4):
                folded = jnp.where(jnp.bitwise_and(rows8, bit) == 0, pltpu.roll(folded, bit, axis=1), folded)
            dw_ref[head, block : block + 1, :] = jnp.sum(folded, axis=0, keepdims=True)
    grad_queries = jnp.concatenate(query_parts, axis=0).T * (1.0 / ROOT_SIZE)
    if given:
        grad_queries = grad_queries + given_ref[...]
    dq_ref[...] = grad_queries.astype(dq_ref.dtype)


def attention_backward(queries, grads, attended, levels, pairs_kv, windows, given=None):
    rows, width = queries.shape
    pairs = HEADS // 2
    pair = 2 * HEAD_DIM
    chunk_spec = pl.BlockSpec((rows, pair), lambda g: (0, g))
    value_spec = pl.BlockSpec((rows, pair), lambda g: (0, g + HEADS // 2))
    window_spec = pl.BlockSpec((2,) + windows.shape[1:], lambda g: (g, 0, 0))
    span = windows.shape[-1]
    extra = [] if given is None else [given]
    return pl.pallas_call(
        functools.partial(attention_backward_kernel, given=given is not None),
        grid=(pairs,),
        in_specs=[chunk_spec] * 3
        + [pl.BlockSpec((1, 2, rows), lambda g: (g, 0, 0))]
        + [chunk_spec] * 2
        + [value_spec] * 2
        + [window_spec]
        + [chunk_spec] * len(extra),
        out_specs=[chunk_spec]
        + [pl.BlockSpec((2, rows, pair), lambda g: (0, 0, g))] * 2
        + [pl.BlockSpec((2, 2, span), lambda g: (g, 0, 0))],
        out_shape=[
            jax.ShapeDtypeStruct((rows, width), F32 if given is None else BF16),
            jax.ShapeDtypeStruct((2, rows, width), F32),
            jax.ShapeDtypeStruct((2, rows, width), BF16),
            jax.ShapeDtypeStruct((HEADS, 2, span), F32),
        ],
        scratch_shapes=[
            pltpu.VMEM((2 * rows, rows), BF16),
            pltpu.VMEM((2 * rows, rows), BF16),
            pltpu.VMEM((2, 8, span), F32),
        ],
        cost_estimate=pl.CostEstimate(
            flops=20 * rows * rows * width, bytes_accessed=36 * rows * width, transcendentals=2 * rows * rows * HEADS
        ),
        name="attention_backward",
    )(queries, grads, attended, levels, *pairs_kv, *pairs_kv, windows, *extra)


def section_swap(value):
    return lax.ppermute(value, SECTION, [(0, 1), (1, 0)])


def inner_swap(value):
    return shift_to(value, INNER, 1)


def outer_swap(value):
    return shift_to(value, OUTER, 1)


def rms_pull(values, gain, grad):
    scale = lax.rsqrt(jnp.mean(values * values, axis=-1, keepdims=True) + EPSILON)
    weighted = grad * gain
    lean = jnp.mean(weighted * values, axis=-1, keepdims=True)
    grad_values = scale * weighted - values * (scale * scale * scale * lean)
    grad_gain = jnp.sum(grad * values * scale, axis=0)
    return grad_values, grad_gain


def send_slots(rows, direction):
    count = lax.axis_size(EXPERT)
    parts = [rows[0]] + [shift_to(rows[k], EXPERT, direction * k) for k in range(1, count)]
    return jnp.concatenate(parts, axis=0)


def route_tables(route, capacity):
    tokens = route.shape[0]
    count = lax.axis_size(EXPERT)
    ahead = jnp.remainder(route - lax.axis_index(EXPERT) + count, count)
    onehot = (ahead[:, :, None] == jnp.arange(count, dtype=jnp.int32)).astype(F32)
    per_row = jnp.sum(onehot, axis=1)
    earlier = (jnp.arange(tokens)[:, None] > jnp.arange(tokens)[None, :]).astype(BF16)
    before = matmul(earlier, per_row.astype(BF16))
    slot_place = jnp.sum(before[:, None, :] * onehot, axis=2).astype(jnp.int32)
    target = ahead * capacity + slot_place
    slots = jnp.arange(count * capacity, dtype=jnp.int32)
    spots = (target[:, 0:1] == slots) | (target[:, 1:2] == slots)
    owner = jnp.remainder(slots // capacity + lax.axis_index(EXPERT), count)
    members = (owner[:, None] == jnp.arange(count, dtype=jnp.int32)).astype(F32)
    return spots, members


def forward(section_in, tables, weights, windows, started):
    spots, members = tables
    slot_table = spots.astype(BF16)
    slot_count = slot_table.shape[1]
    expert_count = lax.axis_size(EXPERT)
    inputs = section_in.astype(F32)
    width = inputs.shape[1]
    if started is None:
        normed = rms_scale(inputs, weights["gain_first"]).astype(BF16)
        pair_own = matmul(normed, weights["pair"]).astype(BF16)
        pair_outer = outer_swap(pair_own)
    else:
        normed, pair_own, pair_outer = started
    pair_inner = inner_swap(pair_own)
    queries = matmul(normed, weights["query"]).astype(BF16)
    pair_both = inner_swap(pair_outer)
    pairs_kv = (pair_own, pair_inner, pair_outer, pair_both)
    attended, attended_full, levels = attention_forward(queries, pairs_kv, windows)
    middle = inputs + matmul(attended, weights["output"])
    mixed_in = rms_scale(middle, weights["gain_second"]).astype(BF16)
    packed = dot_tn(slot_table, mixed_in).astype(BF16)
    arrived = send_slots(packed.reshape(expert_count, -1, width), 1)
    gates_all = softmax_rows(matmul(mixed_in, weights["router"]))
    spread = lax.dot_general(
        gates_all, members, (((1,), (1,)), ((), ())), precision=lax.Precision.HIGHEST, preferred_element_type=F32
    )
    combine = jnp.where(spots, spread, 0.0)
    combine_high = combine.astype(BF16)
    combine_low = (combine - combine_high.astype(F32)).astype(BF16)
    gate_part = matmul(arrived, weights["gate"])
    up_part = matmul(arrived, weights["up"])
    hidden = gated_gelu(gate_part, up_part).astype(BF16)
    produced = dot_nt(hidden, weights["down"]).astype(BF16)
    returned = send_slots(produced.reshape(expert_count, -1, width), -1)
    mixed_out = matmul(combine_high, returned) + matmul(combine_low, returned)
    result = (middle + mixed_out).astype(BF16)
    stored = (
        inputs, normed, queries, pairs_kv, attended, attended_full, levels, middle, mixed_in, gates_all,
        arrived, gate_part, up_part, hidden, returned, combine_high, combine_low,
    )
    return result, stored


def backward(grad_rows, stored, tables, weights, windows, bucket_rows, source, waited):
    spots, members = tables
    slot_table = spots.astype(BF16)
    (
        inputs, normed, queries, pairs_kv, attended, attended_full, levels, middle, mixed_in, gates_all,
        arrived, gate_part, up_part, hidden, returned, combine_high, combine_low,
    ) = stored
    expert_count = lax.axis_size(EXPERT)
    width = inputs.shape[1]
    grad_out = grad_rows.astype(F32)
    grad_slots = (dot_tn(combine_high, grad_rows) + dot_tn(combine_low, grad_rows)).astype(BF16)
    if source == 0:
        grad_slots, arrived = lax.optimization_barrier((grad_slots, arrived))
    received = send_slots(grad_slots.reshape(expert_count, -1, width), 1)
    received, waited[0] = lax.optimization_barrier((received, waited[0]))
    def for_inner(left, right):
        return dot_tn(inner_columns(left, 1), right).astype(BF16)

    def from_inner(term):
        return inner_swap(term).reshape(2, -1, term.shape[1])

    def for_outer(left, right, taken):
        return plus(dot_tn(replica_columns(left, 1), right), take(taken, 1 - lax.axis_index(OUTER), 0))

    down_given, received = lax.optimization_barrier((for_inner(received, hidden), received))
    down_inner = from_inner(down_given)
    grad_hidden = matmul(received, weights["down"])
    unused_value, pull_gelu = jax.vjp(gated_gelu, gate_part, up_part)
    grad_gate, grad_up = pull_gelu(grad_hidden)
    grad_gate, grad_up, down_inner, returned = lax.optimization_barrier(
        (grad_gate.astype(BF16), grad_up.astype(BF16), down_inner, returned)
    )
    products = jnp.where(spots, dot_nt(grad_rows, returned), 0.0)
    grad_gates = jnp.dot(products, members, precision=lax.Precision.HIGHEST, preferred_element_type=F32)
    grad_logits = gates_all * (grad_gates - jnp.sum(gates_all * grad_gates, axis=-1, keepdims=True))
    grad_logits = grad_logits.astype(BF16)
    term_router = dot_tn(mixed_in, grad_logits)

    grad_gate, grad_up, down_given = lax.optimization_barrier(
        (grad_gate, grad_up, for_outer(received, hidden, down_inner))
    )
    down_outer = outer_swap(down_given)
    gate_given, up_given, grad_gate, grad_up = lax.optimization_barrier(
        (for_inner(arrived, grad_gate), for_inner(arrived, grad_up), grad_gate, grad_up)
    )
    gate_inner, up_inner = from_inner(gate_given), from_inner(up_given)
    grad_arrived = (dot_nt(grad_gate, weights["gate"]) + dot_nt(grad_up, weights["up"])).astype(BF16)
    grad_arrived, gate_inner, up_inner = lax.optimization_barrier((grad_arrived, gate_inner, up_inner))
    back_rows = send_slots(grad_arrived.reshape(expert_count, -1, width), -1)
    gate_given = for_outer(arrived, grad_gate, gate_inner)
    up_given = for_outer(arrived, grad_up, up_inner)
    back_rows, gate_given, up_given, down_outer, waited[1], waited[5] = lax.optimization_barrier(
        (back_rows, gate_given, up_given, down_outer, waited[1], waited[5])
    )
    gate_outer = outer_swap(gate_given)
    if source == 1:
        waited[5] = reduce_dense(waited[5])
    share_down = finish_expert(received, hidden, down_inner, down_outer)

    grad_mixed = matmul(slot_table, back_rows) + dot_nt(grad_logits, weights["router"])
    grad_middle, term_second = rms_pull(middle, weights["gain_second"], grad_mixed)
    grad_middle = grad_middle + grad_out
    grad_branch = grad_middle.astype(BF16)
    grad_attended = dot_nt(grad_branch, weights["output"]).astype(BF16)
    term_output = dot_tn(attended, grad_branch).astype(BF16)
    grad_attended, share_down, waited[2] = lax.optimization_barrier((grad_attended, share_down, waited[2]))
    hop_down = lax.ppermute(share_down, SECTION, [(source, 1 - source)])
    grad_part, outer, both, windows_far = attention_backward(
        queries, grad_attended, attended_full, levels, pairs_kv[2:], windows[:, 2:]
    )
    far_taken = inner_swap(both)
    grad_part, far_taken, gate_outer, waited[3] = lax.optimization_barrier(
        (grad_part, far_taken, gate_outer, waited[3])
    )
    passed = plus(outer, far_taken)
    passed, grad_part = lax.optimization_barrier((passed, grad_part))
    outer_sum = outer_swap(passed)
    grad_queries, own, inner, windows_near = attention_backward(
        queries, grad_attended, attended_full, levels, pairs_kv[:2], windows[:, :2], grad_part
    )
    share_gate = finish_expert(arrived, grad_gate, gate_inner, gate_outer)
    even = lax.axis_index(INNER) == 0
    lefts, rights = (attended, normed), (grad_branch, grad_queries)
    given = dot_tn(jnp.where(even, *lefts[::-1]), jnp.where(even, *rights[::-1])).astype(BF16)
    grad_queries, own, inner, outer_sum, share_gate, given, waited[4] = lax.optimization_barrier(
        (grad_queries, own, inner, outer_sum, share_gate, given, waited[4])
    )
    first_taken = inner_swap(given)
    up_given, own = lax.optimization_barrier((up_given, own))
    up_outer = outer_swap(up_given)
    grad_windows = jnp.concatenate([windows_near, windows_far], axis=1)
    near_sum = own + inner_swap(inner).astype(F32)
    grad_windows = grad_windows.reshape(HEADS, -1)
    term_position = lax.dot_general(
        grad_windows, bucket_rows.astype(F32), (((1,), (1,)), ((), ())),
        precision=lax.Precision.HIGHEST, preferred_element_type=F32,
    )
    grad_normed = dot_nt(grad_queries, weights["query"])
    small_early = (term_router, term_second, term_position)
    grad_pair = (near_sum + outer_sum.astype(F32)).astype(BF16)
    index = lax.axis_index(INNER)
    given = dot_tn(normed, take(grad_pair, 1 - index, 0)).astype(BF16)
    grad_pair, grad_normed, first_taken, given, small_early = lax.optimization_barrier(
        (grad_pair, grad_normed, first_taken, given, small_early)
    )
    second_taken = inner_swap(given)
    count = lax.axis_size(EXPERT)
    first_sum = plus(dot_tn(jnp.where(even, *lefts), jnp.where(even, *rights)), first_taken)
    first_sum = first_sum.reshape(2 * count, -1, width)
    grad_normed = grad_normed + dot_nt(grad_pair[0], weights["key"]) + dot_nt(grad_pair[1], weights["value"])
    grad_in, term_first = rms_pull(inputs, weights["gain_first"], grad_normed)
    grad_in = grad_in + grad_middle
    grad_rows = grad_in.astype(BF16)
    small = pack_small(small_early[0], term_first, small_early[1], small_early[2], count).astype(BF16)
    small = small.reshape(2 * count, -1, width)
    small = jnp.pad(small, ((0, 0), (0, 16 - small.shape[1]), (0, 0)))
    second_sum = plus(dot_tn(normed, take(grad_pair, index, 0)), second_taken)
    second_sum = jnp.concatenate([second_sum.reshape(2 * count, -1, width), small], axis=1)
    if source == 0:
        dense = jnp.concatenate([first_sum, second_sum], axis=1)
        grad_rows, dense = lax.optimization_barrier((grad_rows, dense))
    else:
        second_sum, waited[5] = lax.optimization_barrier((second_sum, waited[5]))
        dense = reduce_dense(first_sum)
    share_up = finish_expert(arrived, grad_up, up_inner, up_outer)
    if source == 1:
        hops = [lax.ppermute(value, SECTION, [(1, 0)]) for value in (share_gate, share_up, grad_rows)]
        late, hops = fold_dense(second_sum, hops)
        dense = (dense, late, hops)
    return grad_in, grad_rows, dense, (share_gate, share_up, share_down), hop_down, waited


def reduce_dense(blocks):
    return lax.psum_scatter(blocks, (EXPERT, OUTER), scatter_dimension=0, tiled=False)


def fold_dense(blocks, joined):
    count = lax.axis_size(EXPERT)
    expert_index, outer_index = lax.axis_index(EXPERT), lax.axis_index(OUTER)
    blocks = blocks.reshape(count, 2, -1, blocks.shape[-1])
    part = plus(take(blocks, outer_index, 1), outer_swap(take(blocks, 1 - outer_index, 1)))
    total = take(part, expert_index, 0).astype(F32)
    for ahead in range(1, count):
        given = take(part, jnp.remainder(expert_index + ahead, count), 0)
        total = total + shift_to(given, EXPERT, ahead).astype(F32)
    total, joined = lax.optimization_barrier((total.astype(BF16), joined))
    total = plus(total, lax.ppermute(total, SECTION, [(1, 0)]))
    partner = outer_swap(total)
    lower, even = outer_index == 0, lax.axis_index(INNER) == 0
    own = jnp.where(lower, jnp.stack([total, partner]), jnp.stack([partner, total]))
    other = inner_swap(own)
    return jnp.where(even, jnp.stack([own, other]), jnp.stack([other, own])), joined


def finish_expert(left, right, taken, last):
    return plus(dot_tn(replica_columns(left, 0), right) + take(taken, lax.axis_index(OUTER), 0).astype(F32), last)


def take(blocks, index, axis):
    return lax.dynamic_index_in_dim(blocks, index, axis, keepdims=False)


def plus(left, right):
    return (left.astype(F32) + right.astype(F32)).astype(BF16)


def pick_columns(values, index, size, count):
    parts = [
        lax.dynamic_slice_in_dim(values, start + index * size, size, 1)
        for start in range(0, values.shape[1], size * count)
    ]
    return jnp.concatenate(parts, axis=1)


def inner_columns(values, other):
    return pick_columns(values, jnp.bitwise_xor(lax.axis_index(INNER), other), values.shape[1] // 4, 2)


def replica_columns(values, other):
    width = values.shape[1] // 4
    place = 2 * jnp.bitwise_xor(lax.axis_index(OUTER), other) + lax.axis_index(INNER)
    return lax.dynamic_slice_in_dim(values, place * width, width, 1)


def pack_small(router, first, second, position, count):
    parts = [router.reshape(count, -1), first.reshape(count, -1), second.reshape(count, -1), position.reshape(count, -1)]
    flat = jnp.concatenate(parts, axis=1)
    return jnp.pad(flat, ((0, 0), (0, -flat.shape[1] % 1024)))


def unpack_small(flat, rows, experts, heads, buckets):
    sizes = [rows * experts, rows, rows, heads * buckets]
    starts = [sum(sizes[:k]) for k in range(5)]
    pieces = [flat[:, starts[k] : starts[k + 1]] for k in range(4)]
    return pieces[0].reshape(-1, experts), pieces[1].reshape(-1), pieces[2].reshape(-1), pieces[3].reshape(-1, buckets)


def shards(
    inputs,
    cotangent,
    routes,
    bucket_table,
    query_weight,
    key_weight,
    value_weight,
    output_weight,
    router_weight,
    attention_gain,
    mixture_gain,
    position_bias,
    expert_gate,
    expert_up,
    expert_down,
):
    micro_count = inputs.shape[0]
    tok_rows = inputs.shape[2]
    model_width = inputs.shape[3]
    expert_count = lax.axis_size(EXPERT)
    replica_count = lax.axis_size(OUTER) * lax.axis_size(INNER)
    assert micro_count == lax.axis_size(SECTION) == 2 and replica_count == 4
    capacity = max(2, 9 * tok_rows // (4 * expert_count))
    length = tok_rows * replica_count
    buckets = position_bias.shape[2]
    section_index = lax.axis_index(SECTION)
    replica_index = 2 * lax.axis_index(OUTER) + lax.axis_index(INNER)
    first_section = section_index == 0

    own_rows = lax.dynamic_index_in_dim(inputs[:, 0], section_index, 0, keepdims=False)
    own_cotangent = lax.dynamic_index_in_dim(cotangent[:, 0], section_index, 0, keepdims=False)
    layer_routes = routes[0, :, 0]
    route_kept = lax.dynamic_index_in_dim(layer_routes, section_index, 0, keepdims=False)
    route_given = lax.dynamic_index_in_dim(layer_routes, 1 - section_index, 0, keepdims=False)
    route_taken = section_swap(route_given)
    layer_route = (
        jnp.where(first_section, route_kept, route_taken),
        jnp.where(first_section, route_taken, route_kept),
    )

    dense_rows = query_weight.shape[1]
    inner_index = lax.axis_index(INNER)
    expert_index = lax.axis_index(EXPERT)
    half_rows = dense_rows // 2

    def half_piece(*own_parts):
        return jnp.concatenate(
            [lax.dynamic_slice_in_dim(part, inner_index * half_rows, half_rows, 0) for part in own_parts], axis=1
        )

    def from_first(own):
        return jnp.where(first_section, own, lax.ppermute(own, SECTION, [(0, 1)]))

    def half_of(part, index):
        return lax.dynamic_slice_in_dim(part, index * (part.shape[0] // 2), part.shape[0] // 2, 0)

    def ring_gather(piece, joined=(), at=None):
        whole = jnp.zeros((model_width, piece.shape[1]), BF16)
        for step in range(expert_count):
            start = jnp.remainder(expert_index - step + expert_count, expert_count) * dense_rows
            whole = lax.dynamic_update_slice(whole, piece, (start + inner_index * half_rows, 0))
            whole = lax.dynamic_update_slice(whole, inner_swap(piece), (start + (1 - inner_index) * half_rows, 0))
            if step + 1 < expert_count:
                piece = shift_to(piece, EXPERT, 1)
            if step == at:
                piece, joined = lax.optimization_barrier((piece, joined))
        return whole, joined

    def half_of(part, index):
        return lax.dynamic_slice_in_dim(part, index * (part.shape[0] // 2), part.shape[0] // 2, 0)

    small_own = pack_small(router_weight[0], attention_gain[0], mixture_gain[0], position_bias[0], 1)[0]
    small_taken = section_swap(small_own)
    pair_piece = from_first(half_piece(key_weight[0], value_weight[0]))
    small_piece = jnp.where(
        first_section, jnp.stack([small_own, small_taken]), jnp.stack([small_taken, small_own])
    ).reshape(2, 1, -1)
    small_all = jnp.zeros((2, expert_count, small_piece.shape[2]), BF16)
    for step in range(expert_count):
        source = jnp.remainder(expert_index - step + expert_count, expert_count)
        small_all = lax.dynamic_update_slice(small_all, small_piece, (0, source, 0))
        if step + 1 < expert_count:
            small_piece = shift_to(small_piece, EXPERT, 1)

    second_own, pair_piece = lax.optimization_barrier(
        (half_piece(query_weight[0], output_weight[0]), pair_piece)
    )
    wide_own = (expert_gate[0, 0], expert_up[0, 0], expert_down[0, 0].T)
    wide_kept = jnp.concatenate([half_of(part, section_index) for part in wide_own], axis=1)
    wide_sent = jnp.concatenate([half_of(part, 1 - section_index) for part in wide_own], axis=1)
    wide_sent, pair_piece = lax.optimization_barrier((wide_sent, pair_piece))
    wide_taken = section_swap(wide_sent)
    second_half = from_first(second_own)
    first_pair, wide_taken = ring_gather(pair_piece, wide_taken, expert_count - 2 if expert_count > 1 else 0)
    first_pair, small_all, second_half = lax.optimization_barrier((first_pair, small_all, second_half))
    small_parts = [
        unpack_small(small_all[layer], dense_rows, expert_count, position_bias.shape[1], position_bias.shape[2])
        for layer in range(2)
    ]
    normed = rms_scale(own_rows.astype(F32), small_parts[0][1].astype(F32)).astype(BF16)
    first_own = matmul(normed, first_pair).astype(BF16)
    second_half, first_own = lax.optimization_barrier((second_half, first_own))
    first_outer = outer_swap(first_own)
    second_whole, unused = ring_gather(second_half)
    second_whole, first_outer = lax.optimization_barrier((second_whole, first_outer))
    first_query, first_output = second_whole[:, :model_width], second_whole[:, model_width:]

    eighth = dense_rows // 8

    def by_layer(kept_part, taken_part):
        return jnp.where(first_section, kept_part, taken_part), jnp.where(first_section, taken_part, kept_part)

    dense_axes = (EXPERT, SECTION) + REPLICA

    def eighths(*parts):
        kept_part = jnp.concatenate(
            [lax.dynamic_slice_in_dim(part, (4 * section_index + replica_index) * eighth, eighth, 0) for part in parts],
            axis=1,
        )
        sent_part = jnp.concatenate(
            [lax.dynamic_slice_in_dim(part, (4 * (1 - section_index) + replica_index) * eighth, eighth, 0) for part in parts],
            axis=1,
        )
        return kept_part, sent_part

    hidden_width = expert_gate.shape[3]
    rest_kept, rest_sent = eighths(key_weight[0], value_weight[0], query_weight[0], output_weight[0])
    rest_sent, first_own = lax.optimization_barrier((rest_sent, first_own))
    second_piece = by_layer(rest_kept, section_swap(rest_sent))[1]
    second_piece, first_query, first_own = lax.optimization_barrier((second_piece, first_query, first_own))
    heads_own = position_bias.shape[1]
    wide_pieces = by_layer(wide_kept, wide_taken)
    wide_all = []
    wide_all.append(lax.all_gather(wide_pieces[0], REPLICA + (SECTION,), axis=0, tiled=True))
    second_all = lax.all_gather(second_piece, dense_axes, axis=0, tiled=True)
    wide_all.append(lax.all_gather(wide_pieces[1], REPLICA + (SECTION,), axis=0, tiled=True))
    dense_all = (
        (first_pair, first_query, first_output),
        tuple(second_all[:, a * model_width : z * model_width] for a, z in ((0, 2), (2, 3), (3, 4))),
    )

    reversed_table = jnp.concatenate([jnp.full((1,), -1, jnp.int32), bucket_table[::-1]])
    bucket_onehot = (jnp.arange(buckets, dtype=jnp.int32)[:, None] == reversed_table[None, :]).astype(BF16)
    bucket_rows = jnp.concatenate(
        [
            lax.dynamic_slice(
                bucket_onehot,
                (0, (3 + replica_index - jnp.bitwise_xor(replica_index, ahead)) * tok_rows),
                (buckets, 2 * tok_rows),
            )
            for ahead in range(4)
        ],
        axis=1,
    )

    layers = []
    for layer in range(2):
        router, first, second, position = small_parts[layer]
        weights = dict(
            pair=dense_all[layer][0],
            key=dense_all[layer][0][:, :model_width],
            value=dense_all[layer][0][:, model_width:],
            query=dense_all[layer][1],
            output=dense_all[layer][2],
            router=router,
            gain_first=first.astype(F32),
            gain_second=second.astype(F32),
            gate=wide_all[layer][:, :hidden_width],
            up=wide_all[layer][:, hidden_width : 2 * hidden_width],
            down=wide_all[layer][:, 2 * hidden_width :],
        )
        windows = matmul(position, bucket_rows).reshape(HEADS, 4, 2 * tok_rows)
        layers.append((weights, windows, route_tables(layer_route[layer], capacity)))

    rows, outputs, kept = own_rows, [], []
    for weights, windows, tables in layers:
        rows, stored = forward(rows, tables, weights, windows, (normed, first_own, first_outer) if not kept else None)
        outputs.append(rows)
        kept.append(stored)

    weights, windows, tables = layers[1]
    grad_in_one, grads, dense_one, shares_one, hop_down_one, waited = backward(
        own_cotangent, kept[1], tables, weights, windows, bucket_rows, 0, [()] * 6
    )
    hop_gate_one, hop_up_one = (lax.ppermute(share, SECTION, [(0, 1)]) for share in shares_one[:2])
    grad_from_one = lax.ppermute(grads, SECTION, [(0, 1)])

    weights, windows, tables = layers[0]
    output_taken = section_swap(jnp.where(first_section, outputs[1], outputs[0]))
    waited = [(hop_down_one, output_taken), shares_one, (), hop_gate_one, (), dense_one]
    grad_in_zero, grads, dense_zero, shares_zero, hop_down_zero, waited = backward(
        grads, kept[0], tables, weights, windows, bucket_rows, 1, waited
    )
    (hop_down_one, output_taken), shares_one, unused, hop_gate_one, unused, dense_one = waited
    hops_one = (hop_gate_one, hop_up_one, hop_down_one)
    early_zero, late_zero, (hop_gate_zero, hop_up_zero, grad_from_zero) = dense_zero
    half_count = dense_rows // 2
    early_taken = lax.ppermute(early_zero, SECTION, [(1, 0)])
    one_taken = lax.ppermute(dense_one, SECTION, [(0, 1)])
    early_own = jnp.where(
        first_section, plus(early_zero, early_taken), plus(dense_one[:half_count], one_taken[:half_count])
    )
    dense_own = jnp.concatenate([early_own, plus(dense_one[half_count:], one_taken[half_count:])], axis=0)
    hops_zero = (hop_gate_zero, hop_up_zero, hop_down_zero)
    final_gate, final_up, final_down = (
        jnp.where(first_section, zero, one).astype(F32) + jnp.where(first_section, zero_hop, one_hop).astype(F32)
        for zero, zero_hop, one, one_hop in zip(shares_zero, hops_zero, shares_one, hops_one)
    )
    final_dense = lax.all_gather(dense_own, REPLICA, axis=0, tiled=False).reshape(2, 2, -1, model_width)
    late_own = jnp.where(first_section, late_zero, final_dense[:, :, half_count:].transpose(1, 0, 2, 3))
    final_output, final_query = (
        final_dense[:, inner, :half_count].reshape(dense_rows, model_width).astype(F32) for inner in range(2)
    )
    final_key, final_value = (
        late_own[inner, :, :half_count].reshape(dense_rows, model_width).astype(F32) for inner in range(2)
    )
    small_rows = late_own[:, :, half_count:].astype(F32)
    small_rows = (small_rows[0] + small_rows[1]).reshape(2, -1)
    small_length = small_own.shape[0]
    small_rows = small_rows[:, : small_length // 2].reshape(1, -1)
    final_router, final_first, final_second, final_position = unpack_small(
        small_rows, dense_rows, expert_count, heads_own, buckets
    )

    def both_micros(kept_one, taken_one):
        return jnp.where(
            first_section, jnp.stack([kept_one, taken_one]), jnp.stack([taken_one, kept_one])
        )[None, :, None]

    section_output = both_micros(jnp.where(first_section, outputs[0], outputs[1]), output_taken)
    grad_taken = jnp.where(first_section, grad_from_zero, grad_from_one).astype(F32)
    grad_kept = jnp.where(first_section, grad_in_zero, grad_in_one)
    input_gradient = both_micros(grad_kept, grad_taken)
    return (
        section_output,
        input_gradient,
        final_query[None],
        final_key[None],
        final_value[None],
        final_output[None],
        final_router[None],
        final_first[None],
        final_second[None],
        final_position[None],
        final_gate[None, None],
        final_up[None, None],
        final_down.T[None, None],
    )


def solution(mesh):
    sections, experts, replicas = (mesh.shape[name] for name in ("section", "expert", "replica"))
    fine = Mesh(
        mesh.devices.reshape(sections, experts, replicas // 2, 2), (SECTION, EXPERT, OUTER, INNER)
    )
    rep = REPLICA
    in_specs = (
        P(None, "expert", rep, None),
        P(None, "expert", rep, None),
        P("section", None, "expert", rep, None),
        P(),
        P("section", "expert", None),
        P("section", "expert", None),
        P("section", "expert", None),
        P("section", "expert", None),
        P("section", "expert", None),
        P("section", "expert"),
        P("section", "expert"),
        P("section", "expert", None),
        P("section", "expert", rep, None),
        P("section", "expert", rep, None),
        P("section", "expert", None, rep),
    )
    out_specs = (
        P("section", None, "expert", rep, None),
        P("section", None, "expert", rep, None),
        P("section", "expert", None),
        P("section", "expert", None),
        P("section", "expert", None),
        P("section", "expert", None),
        P("section", "expert", None),
        P("section", "expert"),
        P("section", "expert"),
        P("section", "expert", None),
        P("section", "expert", rep, None),
        P("section", "expert", rep, None),
        P("section", "expert", None, rep),
    )
    return jax.shard_map(shards, mesh=fine, in_specs=in_specs, out_specs=out_specs, check_vma=False)
```

```python
import functools
import math

import jax
import jax.numpy as jnp
from jax import lax
from jax.experimental import pallas as pl
from jax.experimental.pallas import tpu as pltpu
from jax.sharding import Mesh
from jax.sharding import PartitionSpec as P

HEADS = 16
HEAD_DIM = 64
EPSILON = 1e-06
ROOT_SIZE = math.sqrt(HEAD_DIM)

SECTION = "section"
EXPERT = "expert"
OUTER = "outer"
INNER = "inner"
REPLICA = (OUTER, INNER)

BF16 = jnp.bfloat16
F32 = jnp.float32
ROWS = 128


def matmul(left, right):
    return jnp.dot(left, right, preferred_element_type=F32)


def dot_nt(left, right):
    return lax.dot_general(left, right, (((1,), (1,)), ((), ())), preferred_element_type=F32)


def dot_tn(left, right):
    return lax.dot_general(left, right, (((0,), (0,)), ((), ())), preferred_element_type=F32)


def rms_scale(values, gain):
    return values * lax.rsqrt(jnp.mean(values * values, axis=-1, keepdims=True) + EPSILON) * gain


def softmax_rows(scores):
    row_top = jnp.max(scores, axis=-1, keepdims=True)
    expos = jnp.exp(scores - row_top)
    return expos / jnp.sum(expos, axis=-1, keepdims=True)


def gated_gelu(gate_part, up_part):
    return jax.nn.gelu(gate_part, approximate=True) * up_part


def shift_to(value, axis, steps):
    count = lax.axis_size(axis)
    return lax.ppermute(value, axis, [(source, (source + steps) % count) for source in range(count)])


def bias_rows(window, half, queries):
    width = queries + ROWS
    start = ROWS * (1 - half)
    part = jnp.broadcast_to(window[:, start : start + width], (ROWS, width))
    return pltpu.roll(part, width - ROWS, axis=1, stride=1, stride_axis=0)[:, :queries]


def attention_forward_kernel(q_ref, k0, k1, k2, k3, v0, v1, v2, v3, w_ref, o_ref, x_ref, l_ref, s_ref, p_ref):
    queries = q_ref[...]
    count = queries.shape[0]
    lanes = lax.broadcasted_iota(jnp.int32, queries.shape, 1)
    ks, vs = (k0, k1, k2, k3), (v0, v1, v2, v3)
    outs = []
    for head in range(2):
        own = (lanes < HEAD_DIM) if head == 0 else (lanes >= HEAD_DIM)
        q_head = jnp.where(own, queries, jnp.zeros_like(queries)) * jnp.asarray(1.0 / ROOT_SIZE, BF16)
        top = None
        for chunk in range(8):
            block, half = divmod(chunk, 2)
            rows = slice(half * ROWS, (half + 1) * ROWS)
            score = dot_nt(ks[block][rows, :], q_head)
            score = score + bias_rows(w_ref[head, block : block + 1, :], half, count)
            s_ref[chunk * ROWS : (chunk + 1) * ROWS, :] = score
            chunk_top = jnp.max(score, axis=0, keepdims=True)
            top = chunk_top if top is None else jnp.maximum(top, chunk_top)
        total = None
        for chunk in range(8):
            rows = slice(chunk * ROWS, (chunk + 1) * ROWS)
            expo = jnp.exp(s_ref[rows, :] - top)
            p_ref[rows, :] = expo.astype(BF16)
            part = jnp.sum(expo, axis=0, keepdims=True)
            total = part if total is None else total + part
        mixed = None
        for block in range(4):
            part = dot_tn(vs[block][...], p_ref[block * count : (block + 1) * count, :])
            mixed = part if mixed is None else mixed + part
        outs.append(mixed[head * HEAD_DIM : (head + 1) * HEAD_DIM, :] / total)
        l_ref[0, head : head + 1, :] = top + jnp.log(total)
    mixed_rows = jnp.concatenate(outs, axis=0).T
    o_ref[...] = mixed_rows.astype(BF16)
    x_ref[...] = mixed_rows


def attention_forward(queries, pairs_kv, windows):
    rows, width = queries.shape
    pairs = HEADS // 2
    pair = 2 * HEAD_DIM
    chunk_spec = pl.BlockSpec((rows, pair), lambda g: (0, g))
    value_spec = pl.BlockSpec((rows, pair), lambda g: (0, g + HEADS // 2))
    return pl.pallas_call(
        attention_forward_kernel,
        grid=(pairs,),
        in_specs=[chunk_spec] * 5
        + [value_spec] * 4
        + [pl.BlockSpec((2,) + windows.shape[1:], lambda g: (g, 0, 0))],
        out_specs=[chunk_spec, chunk_spec, pl.BlockSpec((1, 2, rows), lambda g: (g, 0, 0))],
        out_shape=[
            jax.ShapeDtypeStruct((rows, width), BF16),
            jax.ShapeDtypeStruct((rows, width), F32),
            jax.ShapeDtypeStruct((pairs, 2, rows), F32),
        ],
        scratch_shapes=[pltpu.VMEM((4 * rows, rows), F32), pltpu.VMEM((4 * rows, rows), BF16)],
        cost_estimate=pl.CostEstimate(
            flops=16 * rows * rows * width, bytes_accessed=20 * rows * width, transcendentals=4 * rows * rows * HEADS
        ),
        name="attention_forward",
    )(queries, *pairs_kv, *pairs_kv, windows)


def attention_backward_kernel(
    q_ref, g_ref, o_ref, l_ref, k0, k1, v0, v1, w_ref, *rest, given
):
    given_ref, rest = (rest[0], rest[1:]) if given else (None, rest)
    dq_ref, dkv0, dkv1, dw_ref, ds_ref, pb_ref, w8_ref = rest
    queries = q_ref[...]
    grads = g_ref[...]
    count = queries.shape[0]
    lanes = lax.broadcasted_iota(jnp.int32, queries.shape, 1)
    ks, vs, dkvs = (k0, k1), (v0, v1), (dkv0, dkv1)
    products = (grads.astype(F32) * o_ref[...]).T
    key_sums, value_sums, query_parts = [None] * 2, [None] * 2, []
    for head in range(2):
        own = (lanes < HEAD_DIM) if head == 0 else (lanes >= HEAD_DIM)
        place_head = slice(head * HEAD_DIM, (head + 1) * HEAD_DIM)
        q_head = jnp.where(own, queries, jnp.zeros_like(queries)) * jnp.asarray(1.0 / ROOT_SIZE, BF16)
        g_head = jnp.where(own, grads, jnp.zeros_like(grads))
        level = l_ref[0, head : head + 1, :]
        row_dot = jnp.sum(products[place_head, :], axis=0, keepdims=True)
        for chunk in range(4):
            block, half = divmod(chunk, 2)
            rows = slice(half * ROWS, (half + 1) * ROWS)
            place = slice(chunk * ROWS, (chunk + 1) * ROWS)
            score = dot_nt(ks[block][rows, :], q_head)
            score = score + bias_rows(w_ref[head, block : block + 1, :], half, count)
            attention = jnp.exp(score - level)
            pb_ref[place, :] = attention.astype(BF16)
            grad_attention = dot_nt(vs[block][rows, :], g_head)
            grad_score = (attention * (grad_attention - row_dot)).astype(BF16)
            ds_ref[place, :] = grad_score
            sheared = jnp.concatenate([grad_score.astype(F32), jnp.zeros((ROWS, ROWS), F32)], axis=1)
            live = ROWS
            while live > 8:
                live = live // 2
                sheared = pltpu.roll(sheared[:live, :], live, axis=1) + sheared[live:, :]
            start = ROWS * (1 - half)
            if half == 0:
                w8_ref[block, :, 0:ROWS] = jnp.zeros((8, ROWS), F32)
                w8_ref[block, :, start : start + count + ROWS] = sheared
            else:
                w8_ref[block, :, start : start + count + ROWS] += sheared
        query_part = None
        for block in range(2):
            place = slice(block * count, (block + 1) * count)
            part = dot_tn(ks[block][...], ds_ref[place, :])
            query_part = part if query_part is None else query_part + part
            key_part = matmul(ds_ref[place, :], q_head)
            value_part = matmul(pb_ref[place, :], g_head)
            if head == 0:
                key_sums[block], value_sums[block] = key_part, value_part
            else:
                dkvs[block][0] = (key_sums[block] + key_part).astype(dkvs[block].dtype)
                dkvs[block][1] = (value_sums[block] + value_part).astype(dkvs[block].dtype)
        query_parts.append(query_part[place_head, :])
        for block in range(2):
            folded = pltpu.roll(w8_ref[block], 1, axis=1)
            rows8 = lax.broadcasted_iota(jnp.int32, folded.shape, 0)
            for bit in (1, 2, 4):
                folded = jnp.where(jnp.bitwise_and(rows8, bit) == 0, pltpu.roll(folded, bit, axis=1), folded)
            dw_ref[head, block : block + 1, :] = jnp.sum(folded, axis=0, keepdims=True)
    grad_queries = jnp.concatenate(query_parts, axis=0).T * (1.0 / ROOT_SIZE)
    if given:
        grad_queries = grad_queries + given_ref[...]
    dq_ref[...] = grad_queries.astype(dq_ref.dtype)


def attention_backward(queries, grads, attended, levels, pairs_kv, windows, given=None):
    rows, width = queries.shape
    pairs = HEADS // 2
    pair = 2 * HEAD_DIM
    chunk_spec = pl.BlockSpec((rows, pair), lambda g: (0, g))
    value_spec = pl.BlockSpec((rows, pair), lambda g: (0, g + HEADS // 2))
    window_spec = pl.BlockSpec((2,) + windows.shape[1:], lambda g: (g, 0, 0))
    span = windows.shape[-1]
    extra = [] if given is None else [given]
    return pl.pallas_call(
        functools.partial(attention_backward_kernel, given=given is not None),
        grid=(pairs,),
        in_specs=[chunk_spec] * 3
        + [pl.BlockSpec((1, 2, rows), lambda g: (g, 0, 0))]
        + [chunk_spec] * 2
        + [value_spec] * 2
        + [window_spec]
        + [chunk_spec] * len(extra),
        out_specs=[chunk_spec]
        + [pl.BlockSpec((2, rows, pair), lambda g: (0, 0, g))] * 2
        + [pl.BlockSpec((2, 2, span), lambda g: (g, 0, 0))],
        out_shape=[
            jax.ShapeDtypeStruct((rows, width), F32 if given is None else BF16),
            jax.ShapeDtypeStruct((2, rows, width), F32),
            jax.ShapeDtypeStruct((2, rows, width), BF16),
            jax.ShapeDtypeStruct((HEADS, 2, span), F32),
        ],
        scratch_shapes=[
            pltpu.VMEM((2 * rows, rows), BF16),
            pltpu.VMEM((2 * rows, rows), BF16),
            pltpu.VMEM((2, 8, span), F32),
        ],
        cost_estimate=pl.CostEstimate(
            flops=20 * rows * rows * width, bytes_accessed=36 * rows * width, transcendentals=2 * rows * rows * HEADS
        ),
        name="attention_backward",
    )(queries, grads, attended, levels, *pairs_kv, *pairs_kv, windows, *extra)


def section_swap(value):
    return lax.ppermute(value, SECTION, [(0, 1), (1, 0)])


def inner_swap(value):
    return shift_to(value, INNER, 1)


def outer_swap(value):
    return shift_to(value, OUTER, 1)


def rms_pull(values, gain, grad):
    scale = lax.rsqrt(jnp.mean(values * values, axis=-1, keepdims=True) + EPSILON)
    weighted = grad * gain
    lean = jnp.mean(weighted * values, axis=-1, keepdims=True)
    grad_values = scale * weighted - values * (scale * scale * scale * lean)
    grad_gain = jnp.sum(grad * values * scale, axis=0)
    return grad_values, grad_gain


def send_slots(rows, direction):
    count = lax.axis_size(EXPERT)
    parts = [rows[0]] + [shift_to(rows[k], EXPERT, direction * k) for k in range(1, count)]
    return jnp.concatenate(parts, axis=0)


def route_tables(route, capacity):
    tokens = route.shape[0]
    count = lax.axis_size(EXPERT)
    ahead = jnp.remainder(route - lax.axis_index(EXPERT) + count, count)
    onehot = (ahead[:, :, None] == jnp.arange(count, dtype=jnp.int32)).astype(F32)
    per_row = jnp.sum(onehot, axis=1)
    earlier = (jnp.arange(tokens)[:, None] > jnp.arange(tokens)[None, :]).astype(BF16)
    before = matmul(earlier, per_row.astype(BF16))
    slot_place = jnp.sum(before[:, None, :] * onehot, axis=2).astype(jnp.int32)
    target = ahead * capacity + slot_place
    slots = jnp.arange(count * capacity, dtype=jnp.int32)
    spots = (target[:, 0:1] == slots) | (target[:, 1:2] == slots)
    owner = jnp.remainder(slots // capacity + lax.axis_index(EXPERT), count)
    members = (owner[:, None] == jnp.arange(count, dtype=jnp.int32)).astype(F32)
    return spots, members


def forward(section_in, tables, weights, windows, started):
    spots, members = tables
    slot_table = spots.astype(BF16)
    slot_count = slot_table.shape[1]
    expert_count = lax.axis_size(EXPERT)
    inputs = section_in.astype(F32)
    width = inputs.shape[1]
    if started is None:
        normed = rms_scale(inputs, weights["gain_first"]).astype(BF16)
        pair_own = matmul(normed, weights["pair"]).astype(BF16)
        pair_outer = outer_swap(pair_own)
    else:
        normed, pair_own, pair_outer = started
    pair_inner = inner_swap(pair_own)
    queries = matmul(normed, weights["query"]).astype(BF16)
    pair_both = inner_swap(pair_outer)
    pairs_kv = (pair_own, pair_inner, pair_outer, pair_both)
    attended, attended_full, levels = attention_forward(queries, pairs_kv, windows)
    middle = inputs + matmul(attended, weights["output"])
    mixed_in = rms_scale(middle, weights["gain_second"]).astype(BF16)
    packed = dot_tn(slot_table, mixed_in).astype(BF16)
    arrived = send_slots(packed.reshape(expert_count, -1, width), 1)
    gates_all = softmax_rows(matmul(mixed_in, weights["router"]))
    spread = lax.dot_general(
        gates_all, members, (((1,), (1,)), ((), ())), precision=lax.Precision.HIGHEST, preferred_element_type=F32
    )
    combine = jnp.where(spots, spread, 0.0)
    combine_high = combine.astype(BF16)
    combine_low = (combine - combine_high.astype(F32)).astype(BF16)
    gate_part = matmul(arrived, weights["gate"])
    up_part = matmul(arrived, weights["up"])
    hidden = gated_gelu(gate_part, up_part).astype(BF16)
    produced = dot_nt(hidden, weights["down"]).astype(BF16)
    returned = send_slots(produced.reshape(expert_count, -1, width), -1)
    mixed_out = matmul(combine_high, returned) + matmul(combine_low, returned)
    result = (middle + mixed_out).astype(BF16)
    stored = (
        inputs, normed, queries, pairs_kv, attended, attended_full, levels, middle, mixed_in, gates_all,
        arrived, gate_part, up_part, hidden, returned, combine_high, combine_low,
    )
    return result, stored


def backward(grad_rows, stored, tables, weights, windows, bucket_rows, source, waited):
    spots, members = tables
    slot_table = spots.astype(BF16)
    (
        inputs, normed, queries, pairs_kv, attended, attended_full, levels, middle, mixed_in, gates_all,
        arrived, gate_part, up_part, hidden, returned, combine_high, combine_low,
    ) = stored
    expert_count = lax.axis_size(EXPERT)
    width = inputs.shape[1]
    grad_out = grad_rows.astype(F32)
    grad_slots = (dot_tn(combine_high, grad_rows) + dot_tn(combine_low, grad_rows)).astype(BF16)
    if source == 0:
        grad_slots, arrived = lax.optimization_barrier((grad_slots, arrived))
    received = send_slots(grad_slots.reshape(expert_count, -1, width), 1)
    received, waited[0] = lax.optimization_barrier((received, waited[0]))
    def for_inner(left, right):
        return dot_tn(inner_columns(left, 1), right).astype(BF16)

    def from_inner(term):
        return inner_swap(term).reshape(2, -1, term.shape[1])

    def for_outer(left, right, taken):
        return plus(dot_tn(replica_columns(left, 1), right), take(taken, 1 - lax.axis_index(OUTER), 0))

    down_given, received = lax.optimization_barrier((for_inner(received, hidden), received))
    down_inner = from_inner(down_given)
    grad_hidden = matmul(received, weights["down"])
    unused_value, pull_gelu = jax.vjp(gated_gelu, gate_part, up_part)
    grad_gate, grad_up = pull_gelu(grad_hidden)
    grad_gate, grad_up, down_inner = lax.optimization_barrier(
        (grad_gate.astype(BF16), grad_up.astype(BF16), down_inner)
    )
    grad_gate, grad_up, down_given = lax.optimization_barrier(
        (grad_gate, grad_up, for_outer(received, hidden, down_inner))
    )
    down_outer = outer_swap(down_given)
    gate_given, up_given, grad_gate, grad_up = lax.optimization_barrier(
        (for_inner(arrived, grad_gate), for_inner(arrived, grad_up), grad_gate, grad_up)
    )
    gate_inner, up_inner = from_inner(gate_given), from_inner(up_given)
    grad_arrived = (dot_nt(grad_gate, weights["gate"]) + dot_nt(grad_up, weights["up"])).astype(BF16)
    grad_arrived, gate_inner, up_inner, returned = lax.optimization_barrier(
        (grad_arrived, gate_inner, up_inner, returned)
    )
    products = jnp.where(spots, dot_nt(grad_rows, returned), 0.0)
    grad_gates = jnp.dot(products, members, precision=lax.Precision.HIGHEST, preferred_element_type=F32)
    grad_logits = gates_all * (grad_gates - jnp.sum(gates_all * grad_gates, axis=-1, keepdims=True))
    grad_logits = grad_logits.astype(BF16)
    term_router = dot_tn(mixed_in, grad_logits)

    back_rows = send_slots(grad_arrived.reshape(expert_count, -1, width), -1)
    gate_given = for_outer(arrived, grad_gate, gate_inner)
    up_given = for_outer(arrived, grad_up, up_inner)
    back_rows, gate_given, up_given, down_outer, waited[1], waited[5] = lax.optimization_barrier(
        (back_rows, gate_given, up_given, down_outer, waited[1], waited[5])
    )
    gate_outer = outer_swap(gate_given)
    if source == 1:
        waited[5] = reduce_dense(waited[5])
    share_down = finish_expert(received, hidden, down_inner, down_outer)

    grad_mixed = matmul(slot_table, back_rows) + dot_nt(grad_logits, weights["router"])
    grad_middle, term_second = rms_pull(middle, weights["gain_second"], grad_mixed)
    grad_middle = grad_middle + grad_out
    grad_branch = grad_middle.astype(BF16)
    grad_attended = dot_nt(grad_branch, weights["output"]).astype(BF16)
    term_output = dot_tn(attended, grad_branch).astype(BF16)
    grad_attended, share_down, waited[2] = lax.optimization_barrier((grad_attended, share_down, waited[2]))
    hop_down = lax.ppermute(share_down, SECTION, [(source, 1 - source)])
    grad_part, outer, both, windows_far = attention_backward(
        queries, grad_attended, attended_full, levels, pairs_kv[2:], windows[:, 2:]
    )
    far_taken = inner_swap(both)
    grad_part, far_taken, gate_outer, waited[3] = lax.optimization_barrier(
        (grad_part, far_taken, gate_outer, waited[3])
    )
    passed = plus(outer, far_taken)
    passed, grad_part = lax.optimization_barrier((passed, grad_part))
    outer_sum = outer_swap(passed)
    grad_queries, own, inner, windows_near = attention_backward(
        queries, grad_attended, attended_full, levels, pairs_kv[:2], windows[:, :2], grad_part
    )
    share_gate = finish_expert(arrived, grad_gate, gate_inner, gate_outer)
    even = lax.axis_index(INNER) == 0
    lefts, rights = (attended, normed), (grad_branch, grad_queries)
    given = dot_tn(jnp.where(even, *lefts[::-1]), jnp.where(even, *rights[::-1])).astype(BF16)
    grad_queries, own, inner, outer_sum, share_gate, given, waited[4] = lax.optimization_barrier(
        (grad_queries, own, inner, outer_sum, share_gate, given, waited[4])
    )
    first_taken = inner_swap(given)
    up_given, own = lax.optimization_barrier((up_given, own))
    up_outer = outer_swap(up_given)
    grad_windows = jnp.concatenate([windows_near, windows_far], axis=1)
    near_sum = own + inner_swap(inner).astype(F32)
    grad_windows = grad_windows.reshape(HEADS, -1)
    term_position = lax.dot_general(
        grad_windows, bucket_rows.astype(F32), (((1,), (1,)), ((), ())),
        precision=lax.Precision.HIGHEST, preferred_element_type=F32,
    )
    grad_normed = dot_nt(grad_queries, weights["query"])
    small_early = (term_router, term_second, term_position)
    grad_pair = (near_sum + outer_sum.astype(F32)).astype(BF16)
    index = lax.axis_index(INNER)
    given = dot_tn(normed, take(grad_pair, 1 - index, 0)).astype(BF16)
    grad_pair, grad_normed, first_taken, given, small_early = lax.optimization_barrier(
        (grad_pair, grad_normed, first_taken, given, small_early)
    )
    second_taken = inner_swap(given)
    count = lax.axis_size(EXPERT)
    first_sum = plus(dot_tn(jnp.where(even, *lefts), jnp.where(even, *rights)), first_taken)
    first_sum = first_sum.reshape(2 * count, -1, width)
    grad_normed = grad_normed + dot_nt(grad_pair[0], weights["key"]) + dot_nt(grad_pair[1], weights["value"])
    grad_in, term_first = rms_pull(inputs, weights["gain_first"], grad_normed)
    grad_in = grad_in + grad_middle
    grad_rows = grad_in.astype(BF16)
    small = pack_small(small_early[0], term_first, small_early[1], small_early[2], count).astype(BF16)
    small = small.reshape(2 * count, -1, width)
    small = jnp.pad(small, ((0, 0), (0, 16 - small.shape[1]), (0, 0)))
    second_sum = plus(dot_tn(normed, take(grad_pair, index, 0)), second_taken)
    second_sum = jnp.concatenate([second_sum.reshape(2 * count, -1, width), small], axis=1)
    if source == 0:
        dense = jnp.concatenate([first_sum, second_sum], axis=1)
        grad_rows, dense = lax.optimization_barrier((grad_rows, dense))
    else:
        second_sum, waited[5] = lax.optimization_barrier((second_sum, waited[5]))
        dense = reduce_dense(first_sum)
    share_up = finish_expert(arrived, grad_up, up_inner, up_outer)
    if source == 1:
        hops = [lax.ppermute(value, SECTION, [(1, 0)]) for value in (share_gate, share_up, grad_rows)]
        late, hops = fold_dense(second_sum, hops)
        dense = (dense, late, hops)
    return grad_in, grad_rows, dense, (share_gate, share_up, share_down), hop_down, waited


def reduce_dense(blocks):
    return lax.psum_scatter(blocks, (EXPERT, OUTER), scatter_dimension=0, tiled=False)


def fold_dense(blocks, joined):
    count = lax.axis_size(EXPERT)
    expert_index, outer_index = lax.axis_index(EXPERT), lax.axis_index(OUTER)
    blocks = blocks.reshape(count, 2, -1, blocks.shape[-1])
    part = plus(take(blocks, outer_index, 1), outer_swap(take(blocks, 1 - outer_index, 1)))
    total = take(part, expert_index, 0).astype(F32)
    for ahead in range(1, count):
        given = take(part, jnp.remainder(expert_index + ahead, count), 0)
        total = total + shift_to(given, EXPERT, ahead).astype(F32)
    total, joined = lax.optimization_barrier((total.astype(BF16), joined))
    total = plus(total, lax.ppermute(total, SECTION, [(1, 0)]))
    partner = outer_swap(total)
    lower, even = outer_index == 0, lax.axis_index(INNER) == 0
    own = jnp.where(lower, jnp.stack([total, partner]), jnp.stack([partner, total]))
    other = inner_swap(own)
    return jnp.where(even, jnp.stack([own, other]), jnp.stack([other, own])), joined


def finish_expert(left, right, taken, last):
    return plus(dot_tn(replica_columns(left, 0), right) + take(taken, lax.axis_index(OUTER), 0).astype(F32), last)


def take(blocks, index, axis):
    return lax.dynamic_index_in_dim(blocks, index, axis, keepdims=False)


def plus(left, right):
    return (left.astype(F32) + right.astype(F32)).astype(BF16)


def pick_columns(values, index, size, count):
    parts = [
        lax.dynamic_slice_in_dim(values, start + index * size, size, 1)
        for start in range(0, values.shape[1], size * count)
    ]
    return jnp.concatenate(parts, axis=1)


def inner_columns(values, other):
    return pick_columns(values, jnp.bitwise_xor(lax.axis_index(INNER), other), values.shape[1] // 4, 2)


def replica_columns(values, other):
    width = values.shape[1] // 4
    place = 2 * jnp.bitwise_xor(lax.axis_index(OUTER), other) + lax.axis_index(INNER)
    return lax.dynamic_slice_in_dim(values, place * width, width, 1)


def pack_small(router, first, second, position, count):
    parts = [router.reshape(count, -1), first.reshape(count, -1), second.reshape(count, -1), position.reshape(count, -1)]
    flat = jnp.concatenate(parts, axis=1)
    return jnp.pad(flat, ((0, 0), (0, -flat.shape[1] % 1024)))


def unpack_small(flat, rows, experts, heads, buckets):
    sizes = [rows * experts, rows, rows, heads * buckets]
    starts = [sum(sizes[:k]) for k in range(5)]
    pieces = [flat[:, starts[k] : starts[k + 1]] for k in range(4)]
    return pieces[0].reshape(-1, experts), pieces[1].reshape(-1), pieces[2].reshape(-1), pieces[3].reshape(-1, buckets)


def shards(
    inputs,
    cotangent,
    routes,
    bucket_table,
    query_weight,
    key_weight,
    value_weight,
    output_weight,
    router_weight,
    attention_gain,
    mixture_gain,
    position_bias,
    expert_gate,
    expert_up,
    expert_down,
):
    micro_count = inputs.shape[0]
    tok_rows = inputs.shape[2]
    model_width = inputs.shape[3]
    expert_count = lax.axis_size(EXPERT)
    replica_count = lax.axis_size(OUTER) * lax.axis_size(INNER)
    assert micro_count == lax.axis_size(SECTION) == 2 and replica_count == 4
    capacity = max(2, 9 * tok_rows // (4 * expert_count))
    length = tok_rows * replica_count
    buckets = position_bias.shape[2]
    section_index = lax.axis_index(SECTION)
    replica_index = 2 * lax.axis_index(OUTER) + lax.axis_index(INNER)
    first_section = section_index == 0

    own_rows = lax.dynamic_index_in_dim(inputs[:, 0], section_index, 0, keepdims=False)
    own_cotangent = lax.dynamic_index_in_dim(cotangent[:, 0], section_index, 0, keepdims=False)
    layer_routes = routes[0, :, 0]
    route_kept = lax.dynamic_index_in_dim(layer_routes, section_index, 0, keepdims=False)
    route_given = lax.dynamic_index_in_dim(layer_routes, 1 - section_index, 0, keepdims=False)
    route_taken = section_swap(route_given)
    layer_route = (
        jnp.where(first_section, route_kept, route_taken),
        jnp.where(first_section, route_taken, route_kept),
    )

    dense_rows = query_weight.shape[1]
    inner_index = lax.axis_index(INNER)
    expert_index = lax.axis_index(EXPERT)
    half_rows = dense_rows // 2

    def half_piece(*own_parts):
        return jnp.concatenate(
            [lax.dynamic_slice_in_dim(part, inner_index * half_rows, half_rows, 0) for part in own_parts], axis=1
        )

    def from_first(own):
        return jnp.where(first_section, own, lax.ppermute(own, SECTION, [(0, 1)]))

    def half_of(part, index):
        return lax.dynamic_slice_in_dim(part, index * (part.shape[0] // 2), part.shape[0] // 2, 0)

    def ring_gather(piece, joined=(), at=None):
        whole = jnp.zeros((model_width, piece.shape[1]), BF16)
        for step in range(expert_count):
            start = jnp.remainder(expert_index - step + expert_count, expert_count) * dense_rows
            whole = lax.dynamic_update_slice(whole, piece, (start + inner_index * half_rows, 0))
            whole = lax.dynamic_update_slice(whole, inner_swap(piece), (start + (1 - inner_index) * half_rows, 0))
            if step + 1 < expert_count:
                piece = shift_to(piece, EXPERT, 1)
            if step == at:
                piece, joined = lax.optimization_barrier((piece, joined))
        return whole, joined

    def half_of(part, index):
        return lax.dynamic_slice_in_dim(part, index * (part.shape[0] // 2), part.shape[0] // 2, 0)

    small_own = pack_small(router_weight[0], attention_gain[0], mixture_gain[0], position_bias[0], 1)[0]
    small_taken = section_swap(small_own)
    pair_piece = from_first(half_piece(key_weight[0], value_weight[0]))
    small_piece = jnp.where(
        first_section, jnp.stack([small_own, small_taken]), jnp.stack([small_taken, small_own])
    ).reshape(2, 1, -1)
    small_all = jnp.zeros((2, expert_count, small_piece.shape[2]), BF16)
    for step in range(expert_count):
        source = jnp.remainder(expert_index - step + expert_count, expert_count)
        small_all = lax.dynamic_update_slice(small_all, small_piece, (0, source, 0))
        if step + 1 < expert_count:
            small_piece = shift_to(small_piece, EXPERT, 1)

    second_own, pair_piece = lax.optimization_barrier(
        (half_piece(query_weight[0], output_weight[0]), pair_piece)
    )
    wide_own = (expert_gate[0, 0], expert_up[0, 0], expert_down[0, 0].T)
    wide_kept = jnp.concatenate([half_of(part, section_index) for part in wide_own], axis=1)
    wide_sent = jnp.concatenate([half_of(part, 1 - section_index) for part in wide_own], axis=1)
    wide_sent, pair_piece = lax.optimization_barrier((wide_sent, pair_piece))
    wide_taken = section_swap(wide_sent)
    second_half = from_first(second_own)
    first_pair, wide_taken = ring_gather(pair_piece, wide_taken, expert_count - 2 if expert_count > 1 else 0)
    first_pair, small_all, second_half = lax.optimization_barrier((first_pair, small_all, second_half))
    small_parts = [
        unpack_small(small_all[layer], dense_rows, expert_count, position_bias.shape[1], position_bias.shape[2])
        for layer in range(2)
    ]
    normed = rms_scale(own_rows.astype(F32), small_parts[0][1].astype(F32)).astype(BF16)
    first_own = matmul(normed, first_pair).astype(BF16)
    second_half, first_own = lax.optimization_barrier((second_half, first_own))
    first_outer = outer_swap(first_own)
    second_whole, unused = ring_gather(second_half)
    second_whole, first_outer = lax.optimization_barrier((second_whole, first_outer))
    first_query, first_output = second_whole[:, :model_width], second_whole[:, model_width:]

    eighth = dense_rows // 8

    def by_layer(kept_part, taken_part):
        return jnp.where(first_section, kept_part, taken_part), jnp.where(first_section, taken_part, kept_part)

    dense_axes = (EXPERT, SECTION) + REPLICA

    def eighths(*parts):
        kept_part = jnp.concatenate(
            [lax.dynamic_slice_in_dim(part, (4 * section_index + replica_index) * eighth, eighth, 0) for part in parts],
            axis=1,
        )
        sent_part = jnp.concatenate(
            [lax.dynamic_slice_in_dim(part, (4 * (1 - section_index) + replica_index) * eighth, eighth, 0) for part in parts],
            axis=1,
        )
        return kept_part, sent_part

    hidden_width = expert_gate.shape[3]
    rest_kept, rest_sent = eighths(key_weight[0], value_weight[0], query_weight[0], output_weight[0])
    rest_sent, first_own = lax.optimization_barrier((rest_sent, first_own))
    second_piece = by_layer(rest_kept, section_swap(rest_sent))[1]
    second_piece, first_query, first_own = lax.optimization_barrier((second_piece, first_query, first_own))
    heads_own = position_bias.shape[1]
    wide_pieces = by_layer(wide_kept, wide_taken)
    wide_all = []
    wide_all.append(lax.all_gather(wide_pieces[0], REPLICA + (SECTION,), axis=0, tiled=True))
    second_all = lax.all_gather(second_piece, dense_axes, axis=0, tiled=True)
    wide_all.append(lax.all_gather(wide_pieces[1], REPLICA + (SECTION,), axis=0, tiled=True))
    dense_all = (
        (first_pair, first_query, first_output),
        tuple(second_all[:, a * model_width : z * model_width] for a, z in ((0, 2), (2, 3), (3, 4))),
    )

    reversed_table = jnp.concatenate([jnp.full((1,), -1, jnp.int32), bucket_table[::-1]])
    bucket_onehot = (jnp.arange(buckets, dtype=jnp.int32)[:, None] == reversed_table[None, :]).astype(BF16)
    bucket_rows = jnp.concatenate(
        [
            lax.dynamic_slice(
                bucket_onehot,
                (0, (3 + replica_index - jnp.bitwise_xor(replica_index, ahead)) * tok_rows),
                (buckets, 2 * tok_rows),
            )
            for ahead in range(4)
        ],
        axis=1,
    )

    layers = []
    for layer in range(2):
        router, first, second, position = small_parts[layer]
        weights = dict(
            pair=dense_all[layer][0],
            key=dense_all[layer][0][:, :model_width],
            value=dense_all[layer][0][:, model_width:],
            query=dense_all[layer][1],
            output=dense_all[layer][2],
            router=router,
            gain_first=first.astype(F32),
            gain_second=second.astype(F32),
            gate=wide_all[layer][:, :hidden_width],
            up=wide_all[layer][:, hidden_width : 2 * hidden_width],
            down=wide_all[layer][:, 2 * hidden_width :],
        )
        windows = matmul(position, bucket_rows).reshape(HEADS, 4, 2 * tok_rows)
        layers.append((weights, windows, route_tables(layer_route[layer], capacity)))

    rows, outputs, kept = own_rows, [], []
    for weights, windows, tables in layers:
        rows, stored = forward(rows, tables, weights, windows, (normed, first_own, first_outer) if not kept else None)
        outputs.append(rows)
        kept.append(stored)

    weights, windows, tables = layers[1]
    grad_in_one, grads, dense_one, shares_one, hop_down_one, waited = backward(
        own_cotangent, kept[1], tables, weights, windows, bucket_rows, 0, [()] * 6
    )
    hop_gate_one, hop_up_one = (lax.ppermute(share, SECTION, [(0, 1)]) for share in shares_one[:2])
    grad_from_one = lax.ppermute(grads, SECTION, [(0, 1)])

    weights, windows, tables = layers[0]
    output_taken = section_swap(jnp.where(first_section, outputs[1], outputs[0]))
    waited = [(hop_down_one, output_taken), shares_one, (), hop_gate_one, (), dense_one]
    grad_in_zero, grads, dense_zero, shares_zero, hop_down_zero, waited = backward(
        grads, kept[0], tables, weights, windows, bucket_rows, 1, waited
    )
    (hop_down_one, output_taken), shares_one, unused, hop_gate_one, unused, dense_one = waited
    hops_one = (hop_gate_one, hop_up_one, hop_down_one)
    early_zero, late_zero, (hop_gate_zero, hop_up_zero, grad_from_zero) = dense_zero
    half_count = dense_rows // 2
    early_taken = lax.ppermute(early_zero, SECTION, [(1, 0)])
    one_taken = lax.ppermute(dense_one, SECTION, [(0, 1)])
    early_own = jnp.where(
        first_section, plus(early_zero, early_taken), plus(dense_one[:half_count], one_taken[:half_count])
    )
    dense_own = jnp.concatenate([early_own, plus(dense_one[half_count:], one_taken[half_count:])], axis=0)
    hops_zero = (hop_gate_zero, hop_up_zero, hop_down_zero)
    final_gate, final_up, final_down = (
        jnp.where(first_section, zero, one).astype(F32) + jnp.where(first_section, zero_hop, one_hop).astype(F32)
        for zero, zero_hop, one, one_hop in zip(shares_zero, hops_zero, shares_one, hops_one)
    )
    final_dense = lax.all_gather(dense_own, REPLICA, axis=0, tiled=False).reshape(2, 2, -1, model_width)
    late_own = jnp.where(first_section, late_zero, final_dense[:, :, half_count:].transpose(1, 0, 2, 3))
    final_output, final_query = (
        final_dense[:, inner, :half_count].reshape(dense_rows, model_width).astype(F32) for inner in range(2)
    )
    final_key, final_value = (
        late_own[inner, :, :half_count].reshape(dense_rows, model_width).astype(F32) for inner in range(2)
    )
    small_rows = late_own[:, :, half_count:].astype(F32)
    small_rows = (small_rows[0] + small_rows[1]).reshape(2, -1)
    small_length = small_own.shape[0]
    small_rows = small_rows[:, : small_length // 2].reshape(1, -1)
    final_router, final_first, final_second, final_position = unpack_small(
        small_rows, dense_rows, expert_count, heads_own, buckets
    )

    def both_micros(kept_one, taken_one):
        return jnp.where(
            first_section, jnp.stack([kept_one, taken_one]), jnp.stack([taken_one, kept_one])
        )[None, :, None]

    section_output = both_micros(jnp.where(first_section, outputs[0], outputs[1]), output_taken)
    grad_taken = jnp.where(first_section, grad_from_zero, grad_from_one).astype(F32)
    grad_kept = jnp.where(first_section, grad_in_zero, grad_in_one)
    input_gradient = both_micros(grad_kept, grad_taken)
    return (
        section_output,
        input_gradient,
        final_query[None],
        final_key[None],
        final_value[None],
        final_output[None],
        final_router[None],
        final_first[None],
        final_second[None],
        final_position[None],
        final_gate[None, None],
        final_up[None, None],
        final_down.T[None, None],
    )


def solution(mesh):
    sections, experts, replicas = (mesh.shape[name] for name in ("section", "expert", "replica"))
    fine = Mesh(
        mesh.devices.reshape(sections, experts, replicas // 2, 2), (SECTION, EXPERT, OUTER, INNER)
    )
    rep = REPLICA
    in_specs = (
        P(None, "expert", rep, None),
        P(None, "expert", rep, None),
        P("section", None, "expert", rep, None),
        P(),
        P("section", "expert", None),
        P("section", "expert", None),
        P("section", "expert", None),
        P("section", "expert", None),
        P("section", "expert", None),
        P("section", "expert"),
        P("section", "expert"),
        P("section", "expert", None),
        P("section", "expert", rep, None),
        P("section", "expert", rep, None),
        P("section", "expert", None, rep),
    )
    out_specs = (
        P("section", None, "expert", rep, None),
        P("section", None, "expert", rep, None),
        P("section", "expert", None),
        P("section", "expert", None),
        P("section", "expert", None),
        P("section", "expert", None),
        P("section", "expert", None),
        P("section", "expert"),
        P("section", "expert"),
        P("section", "expert", None),
        P("section", "expert", rep, None),
        P("section", "expert", rep, None),
        P("section", "expert", None, rep),
    )
    return jax.shard_map(shards, mesh=fine, in_specs=in_specs, out_specs=out_specs, check_vma=False)
```
